768 devices in a mesh: dom: 96 (over z, y_hi, core), sub: 8 (over y_lo, x).
Axes of the slice: x: 4, y: 8 (y_hi: 4, y_lo: 2; y = y_hi * 2 + y_lo), z: 12, core: 2. Of those that a mesh axis runs over, the one named last changes fastest.
Arguments:
- modal_state: float32 [56, 9, 98304], P(None, None, ('dom', 'sub')), may hold values from -6 to 6
- stiffness: float32 [3, 56, 56], replicated, may hold values from -0.75 to 0.75
- jacobians: float32 [3, 9, 9, 98304], P(None, None, None, ('dom', 'sub')), may hold values from -1.25 to 1.25
- flux_solvers: float32 [2, 4, 9, 9, 98304], P(None, None, None, None, ('dom', 'sub')), may hold values from -0.75 to 0.75
- projector: float32 [4, 21, 56], replicated, may hold values from -0.75 to 0.75
- rotations: float32 [3, 21, 21], replicated, may hold values from -1.25 to 1.25
- yield_stress: float32 [98304], P(('dom', 'sub')), may hold values from 0.5 to 8
- cluster: int32 [98304], P(('dom', 'sub')), may hold values from 0 to 1
- orient: int32 [4, 98304], P(None, ('dom', 'sub')), may hold values from 0 to 2
- neighbour_slot: int32 [4, 98304], P(None, ('dom', 'sub')), may hold values from 0 to 703, as said below
- send_map: int32 [147456], P(('dom', 'sub')), may hold values from 0 to 511, as said below
Outputs:
- updated: float32 [56, 9, 98304], P(None, None, ('dom', 'sub'))
The draws below stay inside these ranges and needn't reach their ends.
Inputs may be any that keep to these rules, and one draw needn't show every extreme that they name: `neighbour_slot`: within one partition every received slot 512 + r is named by exactly one face; the other faces name local faces. `send_map`: the 192 entries of one partition are distinct local face numbers.
All inputs are finite; a program needn't handle non-finite values.
Results may differ from the reference program's by a relative error of at most 0.0003.
Values sent between devices are 32-bit elements; how exact they have to be, the bound alone decides.
A program may use at most 64 MiB of HBM per device.

```python
import math
import jax
import jax.numpy as jnp
from jax import lax

BASIS = 56
QUANT = 9
MODES = 21
ORDER = 6
ELEM_DEV = 128
SLOTS_DOM = 64
SLOTS_SUB = 32
ELEMS = 98304
N_DOM = 96
N_SUB = 8


def draw_neighbour_slot(key, part):
    parts_count = ELEMS // ELEM_DEV
    faces_count = 4 * ELEM_DEV
    slot_count = 2 * SLOTS_DOM + 2 * SLOTS_SUB
    keys = jax.random.split(jax.random.fold_in(key, 11), parts_count)

    def one_part(part_key):
        order_key, local_key = jax.random.split(part_key)
        order = jax.random.permutation(order_key, faces_count).astype(jnp.int32)
        local = jax.random.randint(local_key, (faces_count,), 0, faces_count, dtype=jnp.int32)
        ranks = jnp.zeros((faces_count,), jnp.int32).at[order].set(jnp.arange(faces_count, dtype=jnp.int32))
        return jnp.where(ranks < slot_count, faces_count + ranks, local).reshape(4, ELEM_DEV)
    blocks = jax.vmap(one_part)(keys)
    return jnp.transpose(blocks, (1, 0, 2)).reshape(4, ELEMS)


def draw_send_map(key, part):
    parts_count = ELEMS // ELEM_DEV
    faces_count = 4 * ELEM_DEV
    slot_count = 2 * SLOTS_DOM + 2 * SLOTS_SUB
    keys = jax.random.split(jax.random.fold_in(key, 23), parts_count)

    def one_part(part_key):
        first_key, second_key = jax.random.split(part_key)
        chosen = jax.random.permutation(first_key, faces_count - 1)[:slot_count - 1].astype(jnp.int32)
        values = jnp.concatenate([chosen, jnp.full((1,), faces_count - 1, jnp.int32)])
        return jax.random.permutation(second_key, values).astype(jnp.int32)
    return jax.vmap(one_part)(keys).reshape(-1)


def place_ends(values, key, low, largest):
    longest = values.shape.index(max(values.shape))
    spots = []
    for shift in (0, 1):
        where = [jax.random.randint(jax.random.fold_in(key, axis), (), 0, length) for axis, length in enumerate(values.shape)]
        where[longest] = (where[longest] + shift) % values.shape[longest]
        spots.append(tuple(where))
    return values.at[spots[0]].set(low).at[spots[1]].set(largest)


def block_scale(key, extent, shards, low, largest):
    level = 1.0
    for dim, blocks in shards:
        steps = jax.random.uniform(jax.random.fold_in(jax.random.fold_in(key, 6), dim), (blocks,), jnp.float32, low / len(shards), largest / len(shards))
        level = level * jnp.repeat(jnp.exp(steps), extent[dim] // blocks).reshape((-1,) + (1,) * (len(extent) - 1 - dim))
    return level


def noise(key, dims, width, most, cuts=(), kind=jnp.bfloat16):
    factor_of = block_scale(key, dims, cuts, -0.22, 0.18) if cuts else 1.0
    values = jax.random.normal(key, dims, jnp.float32) * width * factor_of
    return jnp.minimum(jnp.maximum(values, -most), most).astype(kind)


def setup_inputs(seed: int = 0) -> dict:
    seeds = jax.random.split(jax.random.key(seed), 12)
    modal_state = noise(seeds[0], (BASIS, QUANT, ELEMS), 1.0, 6.0, ((2, 768),), jnp.float32)
    stiffness = noise(seeds[1], (3, BASIS, BASIS), BASIS ** -0.5, 0.75, (), jnp.float32)
    jacobians = noise(seeds[2], (3, QUANT, QUANT, ELEMS), (3 * QUANT) ** -0.5, 1.25, ((3, 768),), jnp.float32)
    flux_solvers = noise(seeds[3], (2, 4, QUANT, QUANT, ELEMS), (8 * QUANT) ** -0.5, 0.75, ((4, 768),), jnp.float32)
    projector = noise(seeds[4], (4, MODES, BASIS), BASIS ** -0.5, 0.75, (), jnp.float32)
    rotations = noise(seeds[5], (3, MODES, MODES), MODES ** -0.5, 1.25, (), jnp.float32)
    yield_stress = jnp.clip(jnp.exp(math.log(8.0) - 2.7725887 * jax.random.uniform(seeds[6], (ELEMS,), jnp.float32) ** block_scale(seeds[6], (ELEMS,), ((0, 768),), -0.2, 0.2)), 0.5, 8.0)
    cluster = place_ends(jax.random.randint(seeds[7], (ELEMS,), 0, 2), jax.random.fold_in(seeds[7], 1), 0, 1).astype(jnp.int32)
    orient = place_ends(jax.random.randint(seeds[8], (4, ELEMS), 0, 3), jax.random.fold_in(seeds[8], 1), 0, 2).astype(jnp.int32)
    neighbour_slot = draw_neighbour_slot(jax.random.fold_in(seeds[11], 71), 0)
    send_map = draw_send_map(jax.random.fold_in(seeds[11], 71), 0)
    return {"modal_state": modal_state, "stiffness": stiffness, "jacobians": jacobians, "flux_solvers": flux_solvers, "projector": projector, "rotations": rotations, "yield_stress": yield_stress, "cluster": cluster, "orient": orient, "neighbour_slot": neighbour_slot, "send_map": send_map}


exact_dots = lax.Precision.HIGHEST

def derive(current, stiffness, jacobians):
    basis_size = current.shape[0]
    starred = jnp.einsum('bqe,dqpe->dbpe', current, jacobians, precision=exact_dots)
    stacked = jnp.transpose(stiffness, (1, 0, 2)).reshape(basis_size, 3 * basis_size)
    return jnp.dot(stacked, starred.reshape(3 * basis_size, -1), precision=exact_dots).reshape(current.shape)

def predict(state, stiffness, jacobians, both):
    half_one = jnp.zeros_like(state)
    half_two = jnp.zeros_like(state)
    current = state
    for power in range(ORDER):
        factor = float(math.factorial(power + 1))
        half_one = half_one + 1.0 / factor * current
        if both:
            half_two = half_two + (2.0 ** (power + 1) - 1.0) / factor * current
        if power + 1 < ORDER:
            current = derive(current, stiffness, jacobians)
    return (half_one, half_two)

def project(field, projector):
    basis_size, quantities, elem_count = field.shape
    mode_count = projector.shape[1]
    flat = jnp.dot(projector.reshape(4 * mode_count, basis_size), field.reshape(basis_size, quantities * elem_count), precision=exact_dots)
    return flat.reshape(4, mode_count, quantities, elem_count)

def face_table(projected):
    return jnp.transpose(projected, (1, 2, 0, 3)).reshape(projected.shape[1], projected.shape[2], -1)

def neighbours(table, received, neighbour_slot, orient, rotations):
    mode_count, quantities = (table.shape[0], table.shape[1])
    elem_count = neighbour_slot.shape[1]
    extended = jnp.concatenate([table, received], axis=2)
    picked = jnp.take(extended, neighbour_slot.reshape(-1), axis=2)
    turned = jnp.dot(rotations.reshape(3 * mode_count, mode_count), picked.reshape(mode_count, -1), precision=exact_dots)
    turned = turned.reshape(3, mode_count, quantities, 4, elem_count)
    select_mask = (orient[None] == jnp.arange(3, dtype=jnp.int32)[:, None, None]).astype(jnp.float32)
    chosen = lax.optimization_barrier(jnp.sum(turned * select_mask[:, None, None], axis=0))
    return jnp.transpose(chosen, (2, 0, 1, 3))

def update(base, integral, own, near, stiffness, jacobians, flux_solvers, projector):
    basis_size = base.shape[0]
    mode_count = projector.shape[1]
    starred = jnp.einsum('bqe,dqpe->dbpe', integral, jacobians, precision=exact_dots)
    stacked = jnp.transpose(stiffness, (2, 0, 1)).reshape(basis_size, 3 * basis_size)
    volume = jnp.dot(stacked, starred.reshape(3 * basis_size, -1), precision=exact_dots).reshape(base.shape)
    solved = jnp.einsum('fmqe,fqpe->fmpe', own, flux_solvers[0], precision=exact_dots)
    solved = solved + jnp.einsum('fmqe,fqpe->fmpe', near, flux_solvers[1], precision=exact_dots)
    lifted = jnp.dot(projector.reshape(4 * mode_count, basis_size).T, solved.reshape(4 * mode_count, -1), precision=exact_dots)
    return base + volume - lifted.reshape(base.shape)

def yield_back(state, yield_stress):
    normal = state[:, 0:3]
    mean_part = lax.optimization_barrier(jnp.sum(normal, axis=1, keepdims=True)) / 3.0
    spread = normal - mean_part
    shear = state[:, 3:6]
    second_inv = 0.5 * lax.optimization_barrier(jnp.sum(spread[0] ** 2, axis=0)) + lax.optimization_barrier(jnp.sum(shear[0] ** 2, axis=0))
    scaling = yield_stress / jnp.maximum(jnp.sqrt(second_inv), yield_stress)
    return jnp.concatenate([mean_part + scaling * spread, scaling * shear, state[:, 6:]], axis=1)

def split_parts(array, parts):
    shaped = array.reshape(array.shape[:-1] + (parts, array.shape[-1] // parts))
    return jnp.moveaxis(shaped, -2, 0)

def grouped(function, *arrays):
    parts = arrays[0].shape[0]
    group = math.gcd(16, parts)
    shaped = tuple((item.reshape((parts // group, group) + item.shape[1:]) for item in arrays))
    result = lax.map(lambda pieces: jax.vmap(function)(*pieces), shaped)
    return jax.tree.map(lambda item: item.reshape((parts,) + item.shape[2:]), result)

def from_lower(grid, axis):
    if axis == 0:
        return jnp.concatenate([jnp.zeros_like(grid[:1]), grid[:-1]], axis=0)
    return jnp.concatenate([jnp.zeros_like(grid[:, :1]), grid[:, :-1]], axis=1)

def from_upper(grid, axis):
    if axis == 0:
        return jnp.concatenate([grid[1:], jnp.zeros_like(grid[:1])], axis=0)
    return jnp.concatenate([grid[:, 1:], jnp.zeros_like(grid[:, :1])], axis=1)

def deliver(sent):
    grid = sent.reshape((N_DOM, N_SUB) + sent.shape[1:])
    dom_end = 2 * SLOTS_DOM
    sub_mid = dom_end + SLOTS_SUB
    pieces = [from_lower(grid[..., SLOTS_DOM:dom_end], 0), from_upper(grid[..., :SLOTS_DOM], 0), from_lower(grid[..., sub_mid:], 1), from_upper(grid[..., dom_end:sub_mid], 1)]
    return jnp.concatenate(pieces, axis=-1).reshape(sent.shape)

def reference(modal_state, stiffness, jacobians, flux_solvers, projector, rotations, yield_stress, cluster, orient, neighbour_slot, send_map):
    parts = N_DOM * N_SUB
    states = split_parts(modal_state, parts)
    jac_parts = split_parts(jacobians, parts)
    flux_parts = split_parts(flux_solvers, parts)
    yield_parts = split_parts(yield_stress, parts)
    cluster_parts = split_parts(cluster, parts)
    orient_parts = split_parts(orient, parts)
    slot_parts = split_parts(neighbour_slot, parts)
    send_parts = split_parts(send_map, parts)

    def section_one(state, jac, sends):
        half_one, half_two = predict(state, stiffness, jac, True)
        table = face_table(project(half_one, projector))
        return (half_one, half_two, jnp.take(table, sends, axis=2))
    half_one, half_two, sent_one = grouped(section_one, states, jac_parts, send_parts)
    got_one = deliver(sent_one)

    def middle_state(state, first_half, jac, flux, orients, slots, arrived, clusters):
        own = project(first_half, projector)
        near = neighbours(face_table(own), arrived, slots, orients, rotations)
        stepped = update(state, first_half, own, near, stiffness, jac, flux, projector)
        return (jnp.where(clusters[None, None] == 0, stepped, state), near)

    def section_two(state, first_half, second_half, jac, flux, orients, slots, arrived, clusters, sends):
        middle, unused = middle_state(state, first_half, jac, flux, orients, slots, arrived, clusters)
        fine_one, unused_two = predict(middle, stiffness, jac, False)
        late = jnp.where(clusters[None, None] == 0, fine_one, second_half)
        return (fine_one, jnp.take(face_table(project(late, projector)), sends, axis=2))
    fine_one, sent_two = grouped(section_two, states, half_one, half_two, jac_parts, flux_parts, orient_parts, slot_parts, got_one, cluster_parts, send_parts)
    got_two = deliver(sent_two)

    def section_three(state, first_half, second_half, fine_half, jac, flux, yields, clusters, orients, slots, arrived_one, arrived_two):
        middle, near_one = middle_state(state, first_half, jac, flux, orients, slots, arrived_one, clusters)
        fine = clusters[None, None] == 0
        late = jnp.where(fine, fine_half, second_half)
        near_two = neighbours(face_table(project(late, projector)), arrived_two, slots, orients, rotations)
        integral = jnp.where(fine, fine_half, first_half + second_half)
        base = jnp.where(fine, middle, state)
        near = jnp.where(clusters[None, None, None] == 0, near_two, near_one + near_two)
        stepped = update(base, integral, project(integral, projector), near, stiffness, jac, flux, projector)
        return yield_back(stepped, yields)
    result = grouped(section_three, states, half_one, half_two, fine_one, jac_parts, flux_parts, yield_parts, cluster_parts, orient_parts, slot_parts, got_one, got_two)
    return jnp.moveaxis(result, 0, 2).reshape(modal_state.shape)
```

```python
import math

import jax
import jax.numpy as jnp
from jax import lax
from jax.experimental import pallas as pl
from jax.experimental.pallas import tpu as pltpu
from jax.sharding import PartitionSpec as P

ORDER = 6
NB = 56
NQ = 9
NM = 21
MP = 24
NF = 4
NE = 128
SLOTS_DOM = 64
SLOTS_SUB = 32
ROWS = NQ * MP
LANES = NF * NE
HALF = 112
QUARTER = 64
MESH = pl.DeviceIdType.MESH
F32 = jnp.float32
BF16 = jnp.bfloat16


def dot(a, b):
    return jnp.dot(a, b, preferred_element_type=F32)


def dot_t(a, b):
    return lax.dot_general(a, b, (((0,), (0,)), ((), ())), preferred_element_type=F32)


def halves(x):
    high = x.astype(BF16).astype(F32)
    return high, x - high


def split_rows(x):
    high, low = halves(x)
    return jnp.concatenate([high, low, high], axis=0).astype(BF16)


def iota(shape, dim):
    return lax.broadcasted_iota(jnp.int32, shape, dim)


def as_bf16(mask):
    return jnp.where(mask, 1.0, 0.0).astype(BF16)


def split_weights(w):
    k = w.shape[1]
    high, low = halves(w)
    row, col = iota((k, 3 * k), 0), iota((k, 3 * k), 1)
    twice = as_bf16((col == row) | (col == row + k))
    once = as_bf16(col == row + 2 * k)
    return (dot(high.astype(BF16), twice) + dot(low.astype(BF16), once)).astype(BF16)


def split_weights_t(w):
    k = w.shape[0]
    high, low = halves(w)
    row, col = iota((k, 3 * k), 0), iota((k, 3 * k), 1)
    twice = as_bf16((col == row) | (col == row + k))
    once = as_bf16(col == row + 2 * k)
    return (dot_t(high.astype(BF16), twice) + dot_t(low.astype(BF16), once)).astype(BF16)


def split_lift(w):
    high, low = halves(w)
    rows, cols = NF * MP, 3 * NF * MP
    row, col = iota((rows, cols), 0), iota((rows, cols), 1)
    face = (
        (row >= MP).astype(jnp.int32)
        + (row >= 2 * MP).astype(jnp.int32)
        + (row >= 3 * MP).astype(jnp.int32)
    )
    start = row + 2 * MP * face
    twice = as_bf16((col == start) | (col == start + MP))
    once = as_bf16(col == start + 2 * MP)
    return (dot_t(high.astype(BF16), twice) + dot_t(low.astype(BF16), once)).astype(BF16)


def tiles(x):
    return x.reshape(x.shape[0] // 8, 8, x.shape[1])


def flat(x):
    return x.reshape(x.shape[0] * 8, x.shape[2])


def by_power(step, values):
    chosen = jnp.float32(values[-1])
    for index in range(len(values) - 2, -1, -1):
        chosen = jnp.where(step == index, jnp.float32(values[index]), chosen)
    return chosen


def prepare_weights(stiff, proj, rot, w_der, w_vol, w_proj, w_lift, w_rot, padded, padded_rot):
    for d in range(3):
        s = stiff[d]
        w_der[d * NB : (d + 1) * NB, :] = split_weights(s)
        w_vol[d * NB : (d + 1) * NB, :] = split_weights_t(s)
    padded[...] = jnp.zeros_like(padded)
    for m in range(NM):
        for f in range(NF):
            padded[f * MP + m : f * MP + m + 1, :] = proj[m, f : f + 1, :]
    w_proj[...] = split_weights(padded[...])
    w_lift[...] = split_lift(padded[...])
    padded_rot[...] = jnp.zeros_like(padded_rot)
    for o in range(3):
        padded_rot[o * MP : o * MP + NM, 0:NM] = rot[o]
    w_rot[...] = split_weights(padded_rot[...])


def spread_rows(jac, flux, jac_wide, flux_wide):
    for q in range(NQ):
        for p in range(NQ):
            for d in range(3):
                jac_wide[(q * NQ + p) * 3 + d] = jnp.broadcast_to(jac[q, p, d : d + 1, :], (8, NE))
            for s in range(2):
                for f in range(NF):
                    flux_wide[((s * NF + f) * NQ + q) * NQ + p] = jnp.broadcast_to(
                        flux[s, q, p, f : f + 1, :], (8, NE)
                    )


def pick_tables(slot, send_map, spare, picks, packs):
    for f in range(NF):
        want = slot[f : f + 1, :]
        rows = picks.shape[0]
        picks[:, f * NE : (f + 1) * NE] = as_bf16(
            iota((rows, NE), 0) == jnp.broadcast_to(want, (rows, NE))
        )
    lane = iota((8, NE), 1)
    first = jnp.broadcast_to(send_map[0:1, 0:NE], (8, NE))
    turned = pltpu.roll(first, 64, 1)
    spare[:, 0:64] = jnp.broadcast_to(send_map[0:1, NE : NE + 64], (8, 64))
    second = spare[...]
    by = [second] + [pltpu.roll(second, 32 * r, 1) for r in (1, 2, 3)]
    group = (
        (lane >= 32).astype(jnp.int32)
        + (lane >= 64).astype(jnp.int32)
        + (lane >= 96).astype(jnp.int32)
    )

    def four(a, b, c, d):
        return jnp.where(
            group == 0, a, jnp.where(group == 1, b, jnp.where(group == 2, c, d))
        )

    wants = [
        jnp.where(lane < 64, first, turned),
        jnp.where(lane < 64, turned, first),
        four(by[0], by[1], by[2], by[3]),
        four(by[3], by[0], by[1], by[2]),
    ]
    for t in range(4):
        packs[:, t * NE : (t + 1) * NE] = as_bf16(
            iota((LANES, NE), 0) == jnp.broadcast_to(wants[t][0:1, :], (LANES, NE))
        )


def apply_stiffness(weights, fields, out, start, count):
    rhs = jnp.concatenate([split_rows(fields[i]) for i in range(count)], axis=1)
    out[:, start * NE : (start + count) * NE] = dot(weights[...], rhs)


def mix(mats, jac_wide, block):
    totals = [None] * len(block)
    for q in range(NQ):
        for d in range(3):
            t = tiles(mats[d * NB : (d + 1) * NB, q * NE : (q + 1) * NE])
            for i, p in enumerate(block):
                term = t * jac_wide[(q * NQ + p) * 3 + d][None]
                totals[i] = term if totals[i] is None else totals[i] + term
    return [flat(t) for t in totals]


BLOCKS = ((0, 1, 2), (3, 4, 5), (6, 7, 8))


def predict(state, w_der, jac_wide, mats, one, two):
    ones = [1.0 / math.factorial(k + 1) for k in range(ORDER)]
    twos = [(2.0 ** (k + 1) - 1.0) / math.factorial(k + 1) for k in range(ORDER)]
    for block in BLOCKS:
        fields = [state[p] for p in block]
        for p, x in zip(block, fields):
            one[p] = x
            if two is not None:
                two[p] = x
        apply_stiffness(w_der, fields, mats[0], block[0], 3)

    def advance(source, target, c1, c2):
        for block in BLOCKS:
            fields = mix(source, jac_wide, block)
            for p, x in zip(block, fields):
                one[p] = one[p] + c1 * x
                if two is not None:
                    two[p] = two[p] + c2 * x
            if target is not None:
                apply_stiffness(w_der, fields, target, block[0], 3)

    def pair(step, carry):
        advance(mats[0], mats[1], by_power(step, ones[1::2][:2]), by_power(step, twos[1::2][:2]))
        advance(mats[1], mats[0], by_power(step, ones[2::2][:2]), by_power(step, twos[2::2][:2]))
        return carry

    lax.fori_loop(0, 2, pair, 0)
    advance(mats[0], None, ones[5], twos[5])


def project(field, w_proj, table):
    for block in BLOCKS:
        rhs = jnp.concatenate([split_rows(field(p)) for p in block], axis=1)
        faces = dot(w_proj[...], rhs)
        for i, p in enumerate(block):
            for f in range(NF):
                table[p * MP : (p + 1) * MP, f * NE : (f + 1) * NE] = faces[
                    f * MP : (f + 1) * MP, i * NE : (i + 1) * NE
                ]


def pick_local(table, picks, packs, packed, picked):
    high, low = halves(table[...])
    both = jnp.concatenate([high, low], axis=0).astype(BF16)
    got = dot(both, packs[...])
    rows = got[0:ROWS] + got[ROWS : 2 * ROWS]
    lane = iota((HALF, NE), 1)
    zeros = jnp.zeros((256 - ROWS, LANES), F32)
    rows = jnp.concatenate([rows, zeros], axis=0)
    for t in range(2):
        cols = slice(t * NE, (t + 1) * NE)
        packed[t][...] = jnp.where(lane < 64, rows[0:HALF, cols], rows[HALF : 2 * HALF, cols])
    lane = iota((QUARTER, NE), 1)
    for t in range(2, 4):
        cols = slice(t * NE, (t + 1) * NE)
        g = [rows[QUARTER * k : QUARTER * (k + 1), cols] for k in range(4)]
        packed[t][...] = jnp.where(
            lane < 64, jnp.where(lane < 32, g[0], g[1]), jnp.where(lane < 96, g[2], g[3])
        )
    return both


def pick_far(got, picks, picked):
    near_low, near_high, side_low, side_high = [g[...] for g in got]
    lane = iota((HALF, NE), 1)
    top = jnp.where(lane < 64, near_low, pltpu.roll(near_high, 64, 1))
    bottom = jnp.where(lane < 64, pltpu.roll(near_low, 64, 1), near_high)
    dom = jnp.concatenate([top, bottom], axis=0)[0:ROWS]
    lane = iota((QUARTER, NE), 1)
    parts = []
    for k in range(4):
        a = side_low if k == 0 else pltpu.roll(side_low, (128 - 32 * k) % 128, 1)
        b = side_high if k == 1 else pltpu.roll(side_high, (160 - 32 * k) % 128, 1)
        parts.append(jnp.where(lane < 32, a, b))
    sub = jnp.concatenate(parts, axis=0)[0:ROWS]
    far = jnp.concatenate([dom, sub], axis=1)
    high, low = halves(far)
    both = jnp.concatenate([high, low], axis=0).astype(BF16)
    picked[...] = picked[...] + dot(both, picks[LANES : LANES + 2 * NE, :])


def turn(picked, w_rot, orient, q):
    high = picked[q * MP : (q + 1) * MP, :]
    low = picked[ROWS + q * MP : ROWS + (q + 1) * MP, :]
    rhs = jnp.concatenate([high, low, high], axis=0).astype(BF16)
    turned = dot(w_rot[...], rhs)
    out = []
    for f in range(NF):
        which = jnp.broadcast_to(orient[f : f + 1, :], (MP, NE))
        c = slice(f * NE, (f + 1) * NE)
        out.append(
            jnp.where(
                which == 0,
                turned[0:MP, c],
                jnp.where(which == 1, turned[MP : 2 * MP, c], turned[2 * MP : 3 * MP, c]),
            )
        )
    return out


def flux_term(face, flux_wide, side, f, total):
    totals = total
    for q in range(NQ):
        x = tiles(face(q))
        new = []
        for p in range(NQ):
            term = x * flux_wide[((side * NF + f) * NQ + q) * NQ + p][None]
            new.append(term if totals is None else totals[p] + term)
        totals = new
    return totals


def kernel(
    state,
    stiff,
    jac,
    flux,
    proj,
    rot,
    stress,
    cluster,
    orient,
    slot,
    send_map,
    out,
    w_der,
    w_vol,
    w_proj,
    w_lift,
    w_rot,
    padded,
    padded_rot,
    jac_wide,
    flux_wide,
    spare,
    picks,
    packs,
    mats_a,
    mats_b,
    first,
    second,
    middle,
    fine_first,
    table_one,
    table_two,
    picked,
    near,
    lifts,
    lift_in,
    send_a,
    send_b,
    send_c,
    send_d,
    recv_a,
    recv_b,
    recv_c,
    recv_d,
    send_sem,
    recv_sem,
    n_dom,
    n_sub,
):
    i, j = lax.axis_index("dom"), lax.axis_index("sub")
    links = (
        (i > 0, {"dom": i - 1}, 1),
        (i < n_dom - 1, {"dom": i + 1}, 0),
        (j > 0, {"sub": j - 1}, 3),
        (j < n_sub - 1, {"sub": j + 1}, 2),
    )
    sends = (send_a, send_b, send_c, send_d)
    recvs = (recv_a, recv_b, recv_c, recv_d)
    barrier = pltpu.get_barrier_semaphore()
    for there, device, _ in links:

        @pl.when(there)
        def _():
            pl.semaphore_signal(barrier, inc=1, device_id=device, device_id_type=MESH)

    def copy(stage, t):
        return pltpu.make_async_remote_copy(
            src_ref=sends[t].at[stage],
            dst_ref=recvs[links[t][2]].at[stage],
            send_sem=send_sem.at[stage, t],
            recv_sem=recv_sem.at[stage, links[t][2]],
            device_id=links[t][1],
            device_id_type=MESH,
        )

    def arrival(stage, t):
        return pltpu.make_async_remote_copy(
            src_ref=sends[t].at[stage],
            dst_ref=recvs[t].at[stage],
            send_sem=send_sem.at[stage, t],
            recv_sem=recv_sem.at[stage, t],
            device_id=links[t][1],
            device_id_type=MESH,
        )

    def start(stage):
        for t in range(4):

            @pl.when(links[t][0])
            def _():
                copy(stage, t).start()

    def finish(stage):
        for t in range(4):

            @pl.when(links[t][0])
            def _():
                copy(stage, t).wait_send()
                arrival(stage, t).wait_recv()

    prepare_weights(stiff, proj, rot, w_der, w_vol, w_proj, w_lift, w_rot, padded, padded_rot)
    spread_rows(jac, flux, jac_wide, flux_wide)
    pick_tables(slot, send_map, spare, picks, packs)
    for t in range(4):

        @pl.when(jnp.logical_not(links[t][0]))
        def _():
            recvs[t][...] = jnp.zeros_like(recvs[t])

    mats = (mats_a, mats_b)
    predict(state, w_der, jac_wide, mats, first, second)
    project(lambda p: first[p], w_proj, table_one)
    both = pick_local(table_one, picks, packs, [s.at[0] for s in sends], picked)
    peers = sum(there.astype(jnp.int32) for there, _, _ in links)
    pl.semaphore_wait(barrier, peers)
    start(0)
    picked[...] = dot(both, picks[0:LANES, :])
    fine = jnp.broadcast_to(cluster[...], (NB, NE)) == 0
    fine_face = jnp.broadcast_to(cluster[...], (MP, NE)) == 0

    def volume(field, base, target):
        for block in BLOCKS:
            apply_stiffness(w_vol, [field(p) for p in block], mats_a, block[0], 3)
        for block in BLOCKS:
            for p, x in zip(block, mix(mats_a, jac_wide, block)):
                target[p] = base(p) + x

    def own_flux(face):
        for f in range(NF):
            totals = flux_term(lambda q: face(q, f), flux_wide, 0, f, None)
            for p in range(NQ):
                lifts[f * NQ + p] = flat(totals[p])

    def near_flux():
        for f in range(NF):
            totals = flux_term(
                lambda q: near[q, f],
                flux_wide,
                1,
                f,
                [tiles(lifts[f * NQ + p]) for p in range(NQ)],
            )
            for p in range(NQ):
                lift_in[f * 3 * MP : (f + 1) * 3 * MP, p * NE : (p + 1) * NE] = split_rows(
                    flat(totals[p])
                )

    def own_one(q, f):
        return table_one[q * MP : (q + 1) * MP, f * NE : (f + 1) * NE]

    def own_two(q, f):
        late = table_two[q * MP : (q + 1) * MP, f * NE : (f + 1) * NE]
        return jnp.where(fine_face, late, own_one(q, f) + late)

    volume(lambda p: first[p], lambda p: state[p], middle)
    own_flux(own_one)
    finish(0)
    pick_far([r.at[0] for r in recvs], picks, picked)
    for q in range(NQ):
        for f, x in enumerate(turn(picked, w_rot, orient, q)):
            near[q, f] = x
    near_flux()
    lifted = dot(w_lift[...], lift_in[...])
    for p in range(NQ):
        middle[p] = jnp.where(fine, middle[p] - lifted[:, p * NE : (p + 1) * NE], state[p])

    predict(middle, w_der, jac_wide, mats, fine_first, None)
    project(lambda p: jnp.where(fine, fine_first[p], second[p]), w_proj, table_two)
    both = pick_local(table_two, picks, packs, [s.at[1] for s in sends], picked)
    start(1)
    picked[...] = dot(both, picks[0:LANES, :])
    volume(
        lambda p: jnp.where(fine, fine_first[p], first[p] + second[p]),
        lambda p: middle[p],
        middle,
    )
    own_flux(own_two)
    finish(1)
    pick_far([r.at[1] for r in recvs], picks, picked)
    for q in range(NQ):
        for f, x in enumerate(turn(picked, w_rot, orient, q)):
            near[q, f] = jnp.where(fine_face, x, near[q, f] + x)
    near_flux()
    lifted = dot(w_lift[...], lift_in[...])
    stepped = [middle[p] - lifted[:, p * NE : (p + 1) * NE] for p in range(NQ)]
    mean = (stepped[0] + stepped[1] + stepped[2]) / 3.0
    spread = [stepped[p] - mean for p in range(3)]
    lead = [s[0:1] for s in spread] + [stepped[p][0:1] for p in range(3, 6)]
    second_inv = (
        0.5 * (lead[0] * lead[0] + lead[1] * lead[1] + lead[2] * lead[2])
        + lead[3] * lead[3]
        + lead[4] * lead[4]
        + lead[5] * lead[5]
    )
    limit = stress[...]
    scaling = jnp.broadcast_to(limit / jnp.maximum(jnp.sqrt(second_inv), limit), (NB, NE))
    for p in range(3):
        out[p] = mean + scaling * spread[p]
        out[3 + p] = scaling * stepped[3 + p]
        out[6 + p] = stepped[6 + p]


def on_device(n_dom, n_sub, modal_state, stiffness, jacobians, flux_solvers, projector, rotations, yield_stress, cluster, orient, neighbour_slot, send_map):
    vmem = pl.BlockSpec(memory_space=pltpu.VMEM)
    field = pltpu.VMEM((NQ, NB, NE), F32)

    def body(*refs):
        kernel(*refs, n_dom, n_sub)

    result = pl.pallas_call(
        body,
        out_shape=jax.ShapeDtypeStruct((NQ, NB, NE), F32),
        in_specs=[vmem] * 11,
        out_specs=vmem,
        scratch_shapes=[
            pltpu.VMEM((3 * NB, 3 * NB), BF16),
            pltpu.VMEM((3 * NB, 3 * NB), BF16),
            pltpu.VMEM((NF * MP, 3 * NB), BF16),
            pltpu.VMEM((NB, 3 * NF * MP), BF16),
            pltpu.VMEM((3 * MP, 3 * MP), BF16),
            pltpu.VMEM((NF * MP, NB), F32),
            pltpu.VMEM((3 * MP, MP), F32),
            pltpu.VMEM((NQ * NQ * 3, 8, NE), F32),
            pltpu.VMEM((2 * NF * NQ * NQ, 8, NE), F32),
            pltpu.VMEM((8, NE), jnp.int32),
            pltpu.VMEM((LANES + 2 * NE, LANES), BF16),
            pltpu.VMEM((LANES, LANES), BF16),
            pltpu.VMEM((3 * NB, NQ * NE), F32),
            pltpu.VMEM((3 * NB, NQ * NE), F32),
            field,
            field,
            field,
            field,
            pltpu.VMEM((ROWS, LANES), F32),
            pltpu.VMEM((ROWS, LANES), F32),
            pltpu.VMEM((2 * ROWS, LANES), F32),
            pltpu.VMEM((NQ, NF, MP, NE), F32),
            pltpu.VMEM((NF * NQ, MP, NE), F32),
            pltpu.VMEM((3 * NF * MP, NQ * NE), BF16),
            pltpu.VMEM((2, HALF, NE), F32),
            pltpu.VMEM((2, HALF, NE), F32),
            pltpu.VMEM((2, QUARTER, NE), F32),
            pltpu.VMEM((2, QUARTER, NE), F32),
            pltpu.VMEM((2, HALF, NE), F32),
            pltpu.VMEM((2, HALF, NE), F32),
            pltpu.VMEM((2, QUARTER, NE), F32),
            pltpu.VMEM((2, QUARTER, NE), F32),
            pltpu.SemaphoreType.DMA((2, 4)),
            pltpu.SemaphoreType.DMA((2, 4)),
        ],
        compiler_params=pltpu.CompilerParams(
            collective_id=0, has_side_effects=True, vmem_limit_bytes=48 << 20
        ),
    )(
        jnp.transpose(modal_state, (1, 0, 2)),
        stiffness,
        jnp.transpose(jacobians, (1, 2, 0, 3)),
        jnp.transpose(flux_solvers, (0, 2, 3, 1, 4)),
        jnp.transpose(projector, (1, 0, 2)),
        rotations,
        yield_stress.reshape(1, -1),
        cluster.reshape(1, -1),
        orient,
        neighbour_slot,
        send_map.reshape(1, -1),
    )
    return jnp.transpose(result, (1, 0, 2))


def solution(mesh):
    both = ("dom", "sub")
    n_dom, n_sub = mesh.shape["dom"], mesh.shape["sub"]
    placed = (
        P(None, None, both),
        P(),
        P(None, None, None, both),
        P(None, None, None, None, both),
        P(),
        P(),
        P(both),
        P(both),
        P(None, both),
        P(None, both),
        P(both),
    )

    def step(*args):
        return on_device(n_dom, n_sub, *args)

    return jax.shard_map(
        step, mesh=mesh, in_specs=placed, out_specs=P(None, None, both), check_vma=False
    )
```

```python
import math

import jax
import jax.numpy as jnp
from jax import lax
from jax.experimental import pallas as pl
from jax.experimental.pallas import tpu as pltpu
from jax.sharding import PartitionSpec as P

ORDER = 6
NB = 56
NQ = 9
NM = 21
MP = 24
NF = 4
NE = 128
SLOTS_DOM = 64
SLOTS_SUB = 32
ROWS = NQ * MP
LANES = NF * NE
HALF = 112
QUARTER = 64
MESH = pl.DeviceIdType.MESH
F32 = jnp.float32
BF16 = jnp.bfloat16


def dot(a, b):
    return jnp.dot(a, b, preferred_element_type=F32)


def dot_t(a, b):
    return lax.dot_general(a, b, (((0,), (0,)), ((), ())), preferred_element_type=F32)


def halves(x):
    high = x.astype(BF16).astype(F32)
    return high, x - high


def split_rows(x):
    high, low = halves(x)
    return jnp.concatenate([high, low, high], axis=0).astype(BF16)


def iota(shape, dim):
    return lax.broadcasted_iota(jnp.int32, shape, dim)


def as_bf16(mask):
    return jnp.where(mask, 1.0, 0.0).astype(BF16)


def split_weights(w):
    k = w.shape[1]
    high, low = halves(w)
    row, col = iota((k, 3 * k), 0), iota((k, 3 * k), 1)
    twice = as_bf16((col == row) | (col == row + k))
    once = as_bf16(col == row + 2 * k)
    return (dot(high.astype(BF16), twice) + dot(low.astype(BF16), once)).astype(BF16)


def split_weights_t(w):
    k = w.shape[0]
    high, low = halves(w)
    row, col = iota((k, 3 * k), 0), iota((k, 3 * k), 1)
    twice = as_bf16((col == row) | (col == row + k))
    once = as_bf16(col == row + 2 * k)
    return (dot_t(high.astype(BF16), twice) + dot_t(low.astype(BF16), once)).astype(BF16)


def split_lift(w):
    high, low = halves(w)
    rows, cols = NF * MP, 3 * NF * MP
    row, col = iota((rows, cols), 0), iota((rows, cols), 1)
    face = (
        (row >= MP).astype(jnp.int32)
        + (row >= 2 * MP).astype(jnp.int32)
        + (row >= 3 * MP).astype(jnp.int32)
    )
    start = row + 2 * MP * face
    twice = as_bf16((col == start) | (col == start + MP))
    once = as_bf16(col == start + 2 * MP)
    return (dot_t(high.astype(BF16), twice) + dot_t(low.astype(BF16), once)).astype(BF16)


def tiles(x):
    return x.reshape(x.shape[0] // 8, 8, x.shape[1])


def flat(x):
    return x.reshape(x.shape[0] * 8, x.shape[2])


def prepare_derive(stiff, w_der):
    for d in range(3):
        w_der[d * NB : (d + 1) * NB, :] = split_weights(stiff[d])


def prepare_volume(stiff, w_vol):
    for d in range(3):
        w_vol[d * NB : (d + 1) * NB, :] = split_weights_t(stiff[d])


def prepare_faces(proj, w_proj, padded):
    padded[...] = jnp.zeros_like(padded)
    for m in range(NM):
        for f in range(NF):
            padded[f * MP + m : f * MP + m + 1, :] = proj[m, f : f + 1, :]
    w_proj[...] = split_weights(padded[...])


def prepare_turn(rot, w_rot, padded_rot):
    padded_rot[...] = jnp.zeros_like(padded_rot)
    for o in range(3):
        padded_rot[o * MP : o * MP + NM, 0:NM] = rot[o]
    w_rot[...] = split_weights(padded_rot[...])


def spread_jacobians(jac, jac_wide):
    for q in range(NQ):
        for p in range(NQ):
            for d in range(3):
                jac_wide[(q * NQ + p) * 3 + d] = jnp.broadcast_to(jac[q, p, d : d + 1, :], (8, NE))


def spread_flux(flux, flux_wide):
    for q in range(NQ):
        for p in range(NQ):
            for s in range(2):
                for f in range(NF):
                    flux_wide[((s * NF + f) * NQ + q) * NQ + p] = jnp.broadcast_to(
                        flux[s, q, p, f : f + 1, :], (8, NE)
                    )


def pick_columns(slot, picks):
    rows = picks.shape[0]
    for f in range(NF):
        picks[:, f * NE : (f + 1) * NE] = as_bf16(
            iota((rows, NE), 0) == jnp.broadcast_to(slot[f : f + 1, :], (rows, NE))
        )


def pack_columns(send_map, spare, packs):
    lane = iota((8, NE), 1)
    first = jnp.broadcast_to(send_map[0:1, 0:NE], (8, NE))
    turned = pltpu.roll(first, 64, 1)
    spare[:, 0:64] = jnp.broadcast_to(send_map[0:1, NE : NE + 64], (8, 64))
    second = spare[...]
    by = [second] + [pltpu.roll(second, 32 * r, 1) for r in (1, 2, 3)]
    group = (
        (lane >= 32).astype(jnp.int32)
        + (lane >= 64).astype(jnp.int32)
        + (lane >= 96).astype(jnp.int32)
    )

    def four(a, b, c, d):
        return jnp.where(
            group == 0, a, jnp.where(group == 1, b, jnp.where(group == 2, c, d))
        )

    wants = [
        jnp.where(lane < 64, first, turned),
        jnp.where(lane < 64, turned, first),
        four(by[0], by[1], by[2], by[3]),
        four(by[3], by[0], by[1], by[2]),
    ]
    for t in range(4):
        packs[:, t * NE : (t + 1) * NE] = as_bf16(
            iota((LANES, NE), 0) == jnp.broadcast_to(wants[t][0:1, :], (LANES, NE))
        )


def apply_stiffness(weights, fields, out, start, count):
    rhs = jnp.concatenate([split_rows(fields[i]) for i in range(count)], axis=1)
    out[:, start * NE : (start + count) * NE] = dot(weights[...], rhs)


def mix(mats, jac_wide, block):
    totals = [None] * len(block)
    for q in range(NQ):
        for d in range(3):
            t = tiles(mats[d * NB : (d + 1) * NB, q * NE : (q + 1) * NE])
            for i, p in enumerate(block):
                term = t * jac_wide[(q * NQ + p) * 3 + d][None]
                totals[i] = term if totals[i] is None else totals[i] + term
    return [flat(t) for t in totals]


BLOCKS = ((0, 1), (2, 3), (4, 5), (6, 7), (8,))


def predict(state, w_der, jac_wide, mats, one, two):
    ones = [1.0 / math.factorial(k + 1) for k in range(ORDER)]
    twos = [(2.0 ** (k + 1) - 1.0) / math.factorial(k + 1) for k in range(ORDER)]
    for block in BLOCKS:
        fields = [state[p] for p in block]
        for p, x in zip(block, fields):
            one[p] = x
            if two is not None:
                two[p] = x
        apply_stiffness(w_der, fields, mats[0], block[0], len(block))

    def advance(source, target, c1, c2):
        for block in BLOCKS:
            fields = mix(source, jac_wide, block)
            for p, x in zip(block, fields):
                one[p] = one[p] + c1 * x
                if two is not None:
                    two[p] = two[p] + c2 * x
            if target is not None:
                apply_stiffness(w_der, fields, target, block[0], len(block))

    for k in range(1, 5):
        advance(mats[(k + 1) % 2], mats[k % 2], ones[k], twos[k])
    advance(mats[0], None, ones[5], twos[5])


def project(field, w_proj, table):
    for block in BLOCKS:
        rhs = jnp.concatenate([split_rows(field(p)) for p in block], axis=1)
        faces = dot(w_proj[...], rhs)
        for i, p in enumerate(block):
            for f in range(NF):
                table[p * MP : (p + 1) * MP, f * NE : (f + 1) * NE] = faces[
                    f * MP : (f + 1) * MP, i * NE : (i + 1) * NE
                ]


def pick_local(table, picks, packs, packed, picked):
    high, low = halves(table[...])
    both = jnp.concatenate([high, low], axis=0).astype(BF16)
    got = dot(both, packs[...])
    rows = got[0:ROWS] + got[ROWS : 2 * ROWS]
    lane = iota((HALF, NE), 1)
    zeros = jnp.zeros((256 - ROWS, LANES), F32)
    rows = jnp.concatenate([rows, zeros], axis=0)
    for t in range(2):
        cols = slice(t * NE, (t + 1) * NE)
        packed[t][...] = jnp.where(lane < 64, rows[0:HALF, cols], rows[HALF : 2 * HALF, cols])
    lane = iota((QUARTER, NE), 1)
    for t in range(2, 4):
        cols = slice(t * NE, (t + 1) * NE)
        g = [rows[QUARTER * k : QUARTER * (k + 1), cols] for k in range(4)]
        packed[t][...] = jnp.where(
            lane < 64, jnp.where(lane < 32, g[0], g[1]), jnp.where(lane < 96, g[2], g[3])
        )
    return both


def pick_far(got, picks, picked):
    near_low, near_high, side_low, side_high = [g[...] for g in got]
    lane = iota((HALF, NE), 1)
    top = jnp.where(lane < 64, near_low, pltpu.roll(near_high, 64, 1))
    bottom = jnp.where(lane < 64, pltpu.roll(near_low, 64, 1), near_high)
    dom = jnp.concatenate([top, bottom], axis=0)[0:ROWS]
    lane = iota((QUARTER, NE), 1)
    parts = []
    for k in range(4):
        a = side_low if k == 0 else pltpu.roll(side_low, (128 - 32 * k) % 128, 1)
        b = side_high if k == 1 else pltpu.roll(side_high, (160 - 32 * k) % 128, 1)
        parts.append(jnp.where(lane < 32, a, b))
    sub = jnp.concatenate(parts, axis=0)[0:ROWS]
    far = jnp.concatenate([dom, sub], axis=1)
    high, low = halves(far)
    both = jnp.concatenate([high, low], axis=0).astype(BF16)
    picked[...] = picked[...] + dot(both, picks[LANES : LANES + 2 * NE, :])


def turn(picked, w_rot, orient, q):
    high = picked[q * MP : (q + 1) * MP, :]
    low = picked[ROWS + q * MP : ROWS + (q + 1) * MP, :]
    rhs = jnp.concatenate([high, low, high], axis=0).astype(BF16)
    turned = dot(w_rot[...], rhs)
    out = []
    for f in range(NF):
        which = jnp.broadcast_to(orient[f : f + 1, :], (MP, NE))
        c = slice(f * NE, (f + 1) * NE)
        out.append(
            jnp.where(
                which == 0,
                turned[0:MP, c],
                jnp.where(which == 1, turned[MP : 2 * MP, c], turned[2 * MP : 3 * MP, c]),
            )
        )
    return out


def flux_term(face, flux_wide, side, f, total):
    totals = total
    for q in range(NQ):
        x = tiles(face(q))
        new = []
        for p in range(NQ):
            term = x * flux_wide[((side * NF + f) * NQ + q) * NQ + p][None]
            new.append(term if totals is None else totals[p] + term)
        totals = new
    return totals


def kernel(
    state_hbm,
    stiff_hbm,
    jac_hbm,
    flux_hbm,
    proj_hbm,
    rot_hbm,
    stress_hbm,
    cluster_hbm,
    orient_hbm,
    slot_hbm,
    send_map_hbm,
    out,
    state,
    stiff,
    jac,
    flux,
    proj,
    rot,
    stress,
    cluster,
    orient,
    slot,
    send_map,
    load_sem,
    w_der,
    w_vol,
    w_proj,
    w_lift,
    w_rot,
    padded,
    padded_rot,
    jac_wide,
    flux_wide,
    spare,
    picks,
    packs,
    mats_a,
    mats_b,
    first,
    second,
    middle,
    fine_first,
    table_one,
    table_two,
    picked,
    near,
    lifts,
    lift_in,
    send_a,
    send_b,
    send_c,
    send_d,
    recv_a,
    recv_b,
    recv_c,
    recv_d,
    send_sem,
    recv_sem,
    n_dom,
    n_sub,
):
    loads = {
        name: pltpu.make_async_copy(source, target, load_sem.at[index])
        for index, (name, source, target) in enumerate(
            (
                ("stiff", stiff_hbm, stiff),
                ("state", state_hbm, state),
                ("jac", jac_hbm, jac),
                ("proj", proj_hbm, proj),
                ("send_map", send_map_hbm, send_map),
                ("flux", flux_hbm, flux),
                ("slot", slot_hbm, slot),
                ("rot", rot_hbm, rot),
                ("orient", orient_hbm, orient),
                ("cluster", cluster_hbm, cluster),
                ("stress", stress_hbm, stress),
            )
        )
    }
    for load in loads.values():
        load.start()
    i, j = lax.axis_index("dom"), lax.axis_index("sub")
    links = (
        (i > 0, {"dom": i - 1}, 1),
        (i < n_dom - 1, {"dom": i + 1}, 0),
        (j > 0, {"sub": j - 1}, 3),
        (j < n_sub - 1, {"sub": j + 1}, 2),
    )
    sends = (send_a, send_b, send_c, send_d)
    recvs = (recv_a, recv_b, recv_c, recv_d)
    barrier = pltpu.get_barrier_semaphore()
    for there, device, _ in links:

        @pl.when(there)
        def _():
            pl.semaphore_signal(barrier, inc=1, device_id=device, device_id_type=MESH)

    def copy(stage, t):
        return pltpu.make_async_remote_copy(
            src_ref=sends[t].at[stage],
            dst_ref=recvs[links[t][2]].at[stage],
            send_sem=send_sem.at[stage, t],
            recv_sem=recv_sem.at[stage, links[t][2]],
            device_id=links[t][1],
            device_id_type=MESH,
        )

    def arrival(stage, t):
        return pltpu.make_async_remote_copy(
            src_ref=sends[t].at[stage],
            dst_ref=recvs[t].at[stage],
            send_sem=send_sem.at[stage, t],
            recv_sem=recv_sem.at[stage, t],
            device_id=links[t][1],
            device_id_type=MESH,
        )

    def start(stage):
        for t in range(4):

            @pl.when(links[t][0])
            def _():
                copy(stage, t).start()

    def finish(stage):
        for t in range(4):

            @pl.when(links[t][0])
            def _():
                copy(stage, t).wait_send()
                arrival(stage, t).wait_recv()

    loads["stiff"].wait()
    prepare_derive(stiff, w_der)
    loads["jac"].wait()
    spread_jacobians(jac, jac_wide)
    for t in range(4):

        @pl.when(jnp.logical_not(links[t][0]))
        def _():
            recvs[t][...] = jnp.zeros_like(recvs[t])

    mats = (mats_a, mats_b)
    loads["state"].wait()
    predict(state, w_der, jac_wide, mats, first, second)
    loads["proj"].wait()
    prepare_faces(proj, w_proj, padded)
    loads["send_map"].wait()
    pack_columns(send_map, spare, packs)
    project(lambda p: first[p], w_proj, table_one)
    both = pick_local(table_one, picks, packs, [s.at[0] for s in sends], picked)
    peers = sum(there.astype(jnp.int32) for there, _, _ in links)
    pl.semaphore_wait(barrier, peers)
    start(0)
    for name in ("flux", "slot", "rot", "orient", "cluster", "stress"):
        loads[name].wait()
    prepare_volume(stiff, w_vol)
    pick_columns(slot, picks)
    spread_flux(flux, flux_wide)
    w_lift[...] = split_lift(padded[...])
    prepare_turn(rot, w_rot, padded_rot)
    picked[...] = dot(both, picks[0:LANES, :])
    fine = jnp.broadcast_to(cluster[...], (NB, NE)) == 0
    fine_face = jnp.broadcast_to(cluster[...], (MP, NE)) == 0

    def volume(field, base, target):
        for block in BLOCKS:
            apply_stiffness(w_vol, [field(p) for p in block], mats_a, block[0], len(block))
        for block in BLOCKS:
            for p, x in zip(block, mix(mats_a, jac_wide, block)):
                target[p] = base(p) + x

    def own_flux(face):
        for f in range(NF):
            totals = flux_term(lambda q: face(q, f), flux_wide, 0, f, None)
            for p in range(NQ):
                lifts[f * NQ + p] = flat(totals[p])

    def near_flux():
        for f in range(NF):
            totals = flux_term(
                lambda q: near[q, f],
                flux_wide,
                1,
                f,
                [tiles(lifts[f * NQ + p]) for p in range(NQ)],
            )
            for p in range(NQ):
                lift_in[f * 3 * MP : (f + 1) * 3 * MP, p * NE : (p + 1) * NE] = split_rows(
                    flat(totals[p])
                )

    def own_one(q, f):
        return table_one[q * MP : (q + 1) * MP, f * NE : (f + 1) * NE]

    def own_two(q, f):
        late = table_two[q * MP : (q + 1) * MP, f * NE : (f + 1) * NE]
        return jnp.where(fine_face, late, own_one(q, f) + late)

    volume(lambda p: first[p], lambda p: state[p], middle)
    own_flux(own_one)
    finish(0)
    pick_far([r.at[0] for r in recvs], picks, picked)
    for q in range(NQ):
        for f, x in enumerate(turn(picked, w_rot, orient, q)):
            near[q, f] = x
    near_flux()
    lifted = dot(w_lift[...], lift_in[...])
    for p in range(NQ):
        middle[p] = jnp.where(fine, middle[p] - lifted[:, p * NE : (p + 1) * NE], state[p])

    predict(middle, w_der, jac_wide, mats, fine_first, None)
    project(lambda p: jnp.where(fine, fine_first[p], second[p]), w_proj, table_two)
    both = pick_local(table_two, picks, packs, [s.at[1] for s in sends], picked)
    start(1)
    picked[...] = dot(both, picks[0:LANES, :])
    volume(
        lambda p: jnp.where(fine, fine_first[p], first[p] + second[p]),
        lambda p: middle[p],
        middle,
    )
    own_flux(own_two)
    finish(1)
    pick_far([r.at[1] for r in recvs], picks, picked)
    for q in range(NQ):
        for f, x in enumerate(turn(picked, w_rot, orient, q)):
            near[q, f] = jnp.where(fine_face, x, near[q, f] + x)
    near_flux()
    lifted = dot(w_lift[...], lift_in[...])
    stepped = [middle[p] - lifted[:, p * NE : (p + 1) * NE] for p in range(NQ)]
    mean = (stepped[0] + stepped[1] + stepped[2]) / 3.0
    spread = [stepped[p] - mean for p in range(3)]
    lead = [s[0:1] for s in spread] + [stepped[p][0:1] for p in range(3, 6)]
    second_inv = (
        0.5 * (lead[0] * lead[0] + lead[1] * lead[1] + lead[2] * lead[2])
        + lead[3] * lead[3]
        + lead[4] * lead[4]
        + lead[5] * lead[5]
    )
    limit = stress[...]
    scaling = jnp.broadcast_to(limit / jnp.maximum(jnp.sqrt(second_inv), limit), (NB, NE))
    for p in range(3):
        out[p] = mean + scaling * spread[p]
        out[3 + p] = scaling * stepped[3 + p]
        out[6 + p] = stepped[6 + p]


def on_device(n_dom, n_sub, modal_state, stiffness, jacobians, flux_solvers, projector, rotations, yield_stress, cluster, orient, neighbour_slot, send_map):
    vmem = pl.BlockSpec(memory_space=pltpu.VMEM)
    hbm = pl.BlockSpec(memory_space=pltpu.HBM)
    field = pltpu.VMEM((NQ, NB, NE), F32)

    def body(*refs):
        kernel(*refs, n_dom, n_sub)

    wide = lambda x: pltpu.with_memory_space_constraint(x, pltpu.HBM)
    result = pl.pallas_call(
        body,
        out_shape=jax.ShapeDtypeStruct((NQ, NB, NE), F32),
        in_specs=[hbm] * 11,
        out_specs=vmem,
        scratch_shapes=[
            pltpu.VMEM((NQ, NB, NE), F32),
            pltpu.VMEM((3, NB, NB), F32),
            pltpu.VMEM((NQ, NQ, 3, NE), F32),
            pltpu.VMEM((2, NQ, NQ, NF, NE), F32),
            pltpu.VMEM((NM, NF, NB), F32),
            pltpu.VMEM((3, NM, NM), F32),
            pltpu.VMEM((1, NE), F32),
            pltpu.VMEM((1, NE), jnp.int32),
            pltpu.VMEM((NF, NE), jnp.int32),
            pltpu.VMEM((NF, NE), jnp.int32),
            pltpu.VMEM((1, 2 * SLOTS_DOM + 2 * SLOTS_SUB), jnp.int32),
            pltpu.SemaphoreType.DMA((11,)),
            pltpu.VMEM((3 * NB, 3 * NB), BF16),
            pltpu.VMEM((3 * NB, 3 * NB), BF16),
            pltpu.VMEM((NF * MP, 3 * NB), BF16),
            pltpu.VMEM((NB, 3 * NF * MP), BF16),
            pltpu.VMEM((3 * MP, 3 * MP), BF16),
            pltpu.VMEM((NF * MP, NB), F32),
            pltpu.VMEM((3 * MP, MP), F32),
            pltpu.VMEM((NQ * NQ * 3, 8, NE), F32),
            pltpu.VMEM((2 * NF * NQ * NQ, 8, NE), F32),
            pltpu.VMEM((8, NE), jnp.int32),
            pltpu.VMEM((LANES + 2 * NE, LANES), BF16),
            pltpu.VMEM((LANES, LANES), BF16),
            pltpu.VMEM((3 * NB, NQ * NE), F32),
            pltpu.VMEM((3 * NB, NQ * NE), F32),
            field,
            field,
            field,
            field,
            pltpu.VMEM((ROWS, LANES), F32),
            pltpu.VMEM((ROWS, LANES), F32),
            pltpu.VMEM((2 * ROWS, LANES), F32),
            pltpu.VMEM((NQ, NF, MP, NE), F32),
            pltpu.VMEM((NF * NQ, MP, NE), F32),
            pltpu.VMEM((3 * NF * MP, NQ * NE), BF16),
            pltpu.VMEM((2, HALF, NE), F32),
            pltpu.VMEM((2, HALF, NE), F32),
            pltpu.VMEM((2, QUARTER, NE), F32),
            pltpu.VMEM((2, QUARTER, NE), F32),
            pltpu.VMEM((2, HALF, NE), F32),
            pltpu.VMEM((2, HALF, NE), F32),
            pltpu.VMEM((2, QUARTER, NE), F32),
            pltpu.VMEM((2, QUARTER, NE), F32),
            pltpu.SemaphoreType.DMA((2, 4)),
            pltpu.SemaphoreType.DMA((2, 4)),
        ],
        compiler_params=pltpu.CompilerParams(
            collective_id=0, has_side_effects=True, vmem_limit_bytes=48 << 20
        ),
    )(*map(wide, (
        jnp.transpose(modal_state, (1, 0, 2)),
        stiffness,
        jnp.transpose(jacobians, (1, 2, 0, 3)),
        jnp.transpose(flux_solvers, (0, 2, 3, 1, 4)),
        jnp.transpose(projector, (1, 0, 2)),
        rotations,
        yield_stress.reshape(1, -1),
        cluster.reshape(1, -1),
        orient,
        neighbour_slot,
        send_map.reshape(1, -1),
    )))
    return jnp.transpose(result, (1, 0, 2))


def solution(mesh):
    both = ("dom", "sub")
    n_dom, n_sub = mesh.shape["dom"], mesh.shape["sub"]
    placed = (
        P(None, None, both),
        P(),
        P(None, None, None, both),
        P(None, None, None, None, both),
        P(),
        P(),
        P(both),
        P(both),
        P(None, both),
        P(None, both),
        P(both),
    )

    def step(*args):
        return on_device(n_dom, n_sub, *args)

    return jax.shard_map(
        step, mesh=mesh, in_specs=placed, out_specs=P(None, None, both), check_vma=False
    )
```

```python
import math

import jax
import jax.numpy as jnp
from jax import lax
from jax.experimental import pallas as pl
from jax.experimental.pallas import tpu as pltpu
from jax.sharding import PartitionSpec as P

ORDER = 6
NB = 56
NQ = 9
NM = 21
MP = 24
NF = 4
NE = 128
SLOTS_DOM = 64
SLOTS_SUB = 32
ROWS = NQ * MP
LANES = NF * NE
HALF = 112
QUARTER = 64
MESH = pl.DeviceIdType.MESH
F32 = jnp.float32
BF16 = jnp.bfloat16


def dot(a, b):
    return jnp.dot(a, b, preferred_element_type=F32)


def dot_t(a, b):
    return lax.dot_general(a, b, (((0,), (0,)), ((), ())), preferred_element_type=F32)


def dot_rows(a, b):
    return lax.dot_general(a, b, (((1,), (1,)), ((), ())), preferred_element_type=F32)


def halves(x):
    high = x.astype(BF16).astype(F32)
    return high, x - high


def split_rows(x):
    high, low = halves(x)
    return jnp.concatenate([high, low, high], axis=0).astype(BF16)


def iota(shape, dim):
    return lax.broadcasted_iota(jnp.int32, shape, dim)


def as_bf16(mask):
    return jnp.where(mask, 1.0, 0.0).astype(BF16)


def split_weights(w):
    k = w.shape[1]
    high, low = halves(w)
    row, col = iota((k, 3 * k), 0), iota((k, 3 * k), 1)
    twice = as_bf16((col == row) | (col == row + k))
    once = as_bf16(col == row + 2 * k)
    return (dot(high.astype(BF16), twice) + dot(low.astype(BF16), once)).astype(BF16)


def split_weights_t(w):
    k = w.shape[0]
    high, low = halves(w)
    row, col = iota((k, 3 * k), 0), iota((k, 3 * k), 1)
    twice = as_bf16((col == row) | (col == row + k))
    once = as_bf16(col == row + 2 * k)
    return (dot_t(high.astype(BF16), twice) + dot_t(low.astype(BF16), once)).astype(BF16)


def split_lift(w):
    high, low = halves(w)
    rows, cols = NF * MP, 3 * NF * MP
    row, col = iota((rows, cols), 0), iota((rows, cols), 1)
    face = (
        (row >= MP).astype(jnp.int32)
        + (row >= 2 * MP).astype(jnp.int32)
        + (row >= 3 * MP).astype(jnp.int32)
    )
    start = row + 2 * MP * face
    twice = as_bf16((col == start) | (col == start + MP))
    once = as_bf16(col == start + 2 * MP)
    return (dot_t(high.astype(BF16), twice) + dot_t(low.astype(BF16), once)).astype(BF16)


def tiles(x):
    return x.reshape(x.shape[0] // 8, 8, x.shape[1])


def flat(x):
    return x.reshape(x.shape[0] * 8, x.shape[2])


def prepare_derive(stiff, w_der):
    for d in range(3):
        w_der[d * NB : (d + 1) * NB, :] = split_weights(stiff[d])


def prepare_volume(stiff, w_vol):
    for d in range(3):
        w_vol[d * NB : (d + 1) * NB, :] = split_weights_t(stiff[d])


def prepare_faces(proj, w_proj, padded):
    padded[...] = jnp.zeros_like(padded)
    for m in range(NM):
        for f in range(NF):
            padded[f * MP + m : f * MP + m + 1, :] = proj[m, f : f + 1, :]
    w_proj[...] = split_weights(padded[...])


def prepare_turn(rot, w_rot, padded_rot):
    padded_rot[...] = jnp.zeros_like(padded_rot)
    for o in range(3):
        padded_rot[o * MP : o * MP + NM, 0:NM] = rot[o]
    w_rot[...] = split_weights(padded_rot[...])


def spread_jacobians(jac, jac_wide):
    for q in range(NQ):
        for p in range(NQ):
            for d in range(3):
                jac_wide[(q * NQ + p) * 3 + d] = jnp.broadcast_to(jac[q, p, d : d + 1, :], (8, NE))


def spread_flux(flux, flux_wide):
    for q in range(NQ):
        for p in range(NQ):
            for s in range(2):
                for f in range(NF):
                    flux_wide[((s * NF + f) * NQ + q) * NQ + p] = jnp.broadcast_to(
                        flux[s, q, p, f : f + 1, :], (8, NE)
                    )


def pick_columns(slot, picks):
    rows = picks.shape[0]
    for f in range(NF):
        picks[:, f * NE : (f + 1) * NE] = as_bf16(
            iota((rows, NE), 0) == jnp.broadcast_to(slot[f : f + 1, :], (rows, NE))
        )


def pack_columns(send_map, spare, packs):
    lane = iota((8, NE), 1)
    first = jnp.broadcast_to(send_map[0:1, 0:NE], (8, NE))
    turned = pltpu.roll(first, 64, 1)
    spare[:, 0:64] = jnp.broadcast_to(send_map[0:1, NE : NE + 64], (8, 64))
    second = spare[...]
    by = [second] + [pltpu.roll(second, 32 * r, 1) for r in (1, 2, 3)]
    group = (
        (lane >= 32).astype(jnp.int32)
        + (lane >= 64).astype(jnp.int32)
        + (lane >= 96).astype(jnp.int32)
    )

    def four(a, b, c, d):
        return jnp.where(
            group == 0, a, jnp.where(group == 1, b, jnp.where(group == 2, c, d))
        )

    wants = [
        jnp.where(lane < 64, first, turned),
        jnp.where(lane < 64, turned, first),
        four(by[0], by[1], by[2], by[3]),
        four(by[3], by[0], by[1], by[2]),
    ]
    for t in range(4):
        packs[:, t * NE : (t + 1) * NE] = as_bf16(
            iota((LANES, NE), 0) == jnp.broadcast_to(wants[t][0:1, :], (LANES, NE))
        )


def apply_stiffness(weights, fields, out, start, count):
    rhs = jnp.concatenate([split_rows(fields[i]) for i in range(count)], axis=1)
    out[:, start * NE : (start + count) * NE] = dot(weights[...], rhs)


def mix(mats, jac_wide, block):
    totals = [None] * len(block)
    for q in range(NQ):
        for d in range(3):
            t = tiles(mats[d * NB : (d + 1) * NB, q * NE : (q + 1) * NE])
            for i, p in enumerate(block):
                term = t * jac_wide[(q * NQ + p) * 3 + d][None]
                totals[i] = term if totals[i] is None else totals[i] + term
    return [flat(t) for t in totals]


BLOCKS = ((0, 1), (2, 3), (4, 5), (6, 7), (8,))


ONES = [1.0 / math.factorial(k + 1) for k in range(ORDER)]
TWOS = [(2.0 ** (k + 1) - 1.0) / math.factorial(k + 1) for k in range(ORDER)]


def predict(state, w_der, jac_wide, mats, one, kept, done):
    for block in BLOCKS:
        fields = [state[p] for p in block]
        for p, x in zip(block, fields):
            one[p] = x
        apply_stiffness(w_der, fields, mats[0], block[0], len(block))

    for k in range(1, ORDER):
        source, target = mats[(k + 1) % 2], mats[k % 2]
        for block in BLOCKS:
            fields = mix(source, jac_wide, block)
            for p, x in zip(block, fields):
                one[p] = one[p] + ONES[k] * x
                if kept is not None:
                    kept[k - 1, p] = x
            if k + 1 < ORDER:
                apply_stiffness(w_der, fields, target, block[0], len(block))
            else:
                done(block)


def later(state, kept, two):
    for p in range(NQ):
        total = state[p]
        for k in range(1, ORDER):
            total = total + TWOS[k] * kept[k - 1, p]
        two[p] = total


def project(fields, block, w_proj, table):
    rhs = jnp.concatenate([split_rows(x) for x in fields], axis=1)
    faces = dot(w_proj[...], rhs)
    for i, p in enumerate(block):
        for f in range(NF):
            table[p * MP : (p + 1) * MP, f * NE : (f + 1) * NE] = faces[
                f * MP : (f + 1) * MP, i * NE : (i + 1) * NE
            ]


def pick_local(table, picks, packs, packed, picked):
    high, low = halves(table[...])
    both = jnp.concatenate([high, low], axis=0).astype(BF16)
    got = dot(both, packs[...])
    rows = got[0:ROWS] + got[ROWS : 2 * ROWS]
    lane = iota((HALF, NE), 1)
    zeros = jnp.zeros((256 - ROWS, LANES), F32)
    rows = jnp.concatenate([rows, zeros], axis=0)
    for t in range(2):
        cols = slice(t * NE, (t + 1) * NE)
        packed[t][...] = jnp.where(lane < 64, rows[0:HALF, cols], rows[HALF : 2 * HALF, cols])
    lane = iota((QUARTER, NE), 1)
    for t in range(2, 4):
        cols = slice(t * NE, (t + 1) * NE)
        g = [rows[QUARTER * k : QUARTER * (k + 1), cols] for k in range(4)]
        packed[t][...] = jnp.where(
            lane < 64, jnp.where(lane < 32, g[0], g[1]), jnp.where(lane < 96, g[2], g[3])
        )
    return both


def far_rows(got):
    near_low, near_high, side_low, side_high = [g[...] for g in got]
    lane = iota((HALF, NE), 1)
    top = jnp.where(lane < 64, near_low, pltpu.roll(near_high, 64, 1))
    bottom = jnp.where(lane < 64, pltpu.roll(near_low, 64, 1), near_high)
    dom = jnp.concatenate([top, bottom], axis=0)[0:ROWS]
    lane = iota((QUARTER, NE), 1)
    parts = []
    for k in range(4):
        a = side_low if k == 0 else pltpu.roll(side_low, (128 - 32 * k) % 128, 1)
        b = side_high if k == 1 else pltpu.roll(side_high, (160 - 32 * k) % 128, 1)
        parts.append(jnp.where(lane < 32, a, b))
    sub = jnp.concatenate(parts, axis=0)[0:ROWS]
    far = jnp.concatenate([dom, sub], axis=1)
    return halves(far)


def prepare_slots(flux, orient, picks, rows, lines, slot_flux, slot_turn):
    rows[80:88, :] = jnp.zeros((8, LANES), F32)
    for q in range(NQ):
        for p in range(NQ):
            for f in range(NF):
                rows[q * NQ + p : q * NQ + p + 1, f * NE : (f + 1) * NE] = flux[
                    1, q, p, f : f + 1, :
                ]
    high, low = halves(rows[...])
    both = jnp.concatenate([high, low], axis=0).astype(BF16)
    far = picks[LANES : LANES + 2 * NE, :]
    got = dot_rows(both, far)
    for index in range(NQ * NQ):
        line = got[index : index + 1, :] + got[88 + index : 89 + index, :]
        slot_flux[index] = jnp.broadcast_to(line, (8, 2 * NE))
    for f in range(NF):
        lines[:, f * NE : (f + 1) * NE] = jnp.broadcast_to(
            orient[f : f + 1, :].astype(F32), (8, NE)
        )
    slot_turn[...] = dot_rows(lines[...].astype(BF16), far)


def far_update(got, w_rot, w_lift, picks, slot_flux, slot_turn, turned, sums, lift_in):
    high, low = far_rows(got)
    which = slot_turn[...][None]
    for q in range(NQ):
        h, l = high[q * MP : (q + 1) * MP], low[q * MP : (q + 1) * MP]
        r = dot(w_rot[...], jnp.concatenate([h, l, h], axis=0).astype(BF16))
        r = [tiles(r[o * MP : (o + 1) * MP]) for o in range(3)]
        turned[q] = flat(jnp.where(which < 0.5, r[0], jnp.where(which < 1.5, r[1], r[2])))
    for block in ((0, 1, 2), (3, 4, 5), (6, 7, 8)):
        totals = [None] * len(block)
        for q in range(NQ):
            x = tiles(turned[q])
            for i, p in enumerate(block):
                term = x * slot_flux[q * NQ + p][None]
                totals[i] = term if totals[i] is None else totals[i] + term
        for i, p in enumerate(block):
            sums[p * MP : (p + 1) * MP, :] = flat(totals[i])
    high, low = halves(sums[...])
    both = jnp.concatenate([high, low], axis=0).astype(BF16)
    back = dot(both, picks[LANES : LANES + 2 * NE, :])
    for f in range(NF):
        c = slice(f * NE, (f + 1) * NE)
        for p in range(NQ):
            h = back[p * MP : (p + 1) * MP, c]
            l = back[ROWS + p * MP : ROWS + (p + 1) * MP, c]
            lift_in[f * 3 * MP : (f + 1) * 3 * MP, p * NE : (p + 1) * NE] = jnp.concatenate(
                [h, l, h], axis=0
            ).astype(BF16)
    return dot(w_lift[...], lift_in[...])


def turn(picked, w_rot, orient, q):
    high = picked[q * MP : (q + 1) * MP, :]
    low = picked[ROWS + q * MP : ROWS + (q + 1) * MP, :]
    rhs = jnp.concatenate([high, low, high], axis=0).astype(BF16)
    turned = dot(w_rot[...], rhs)
    out = []
    for f in range(NF):
        which = jnp.broadcast_to(orient[f : f + 1, :], (MP, NE))
        c = slice(f * NE, (f + 1) * NE)
        out.append(
            jnp.where(
                which == 0,
                turned[0:MP, c],
                jnp.where(which == 1, turned[MP : 2 * MP, c], turned[2 * MP : 3 * MP, c]),
            )
        )
    return out


def flux_term(face, flux_wide, side, f, total):
    totals = total
    for q in range(NQ):
        x = tiles(face(q))
        new = []
        for p in range(NQ):
            term = x * flux_wide[((side * NF + f) * NQ + q) * NQ + p][None]
            new.append(term if totals is None else totals[p] + term)
        totals = new
    return totals


def kernel(
    state_hbm,
    stiff_hbm,
    jac_hbm,
    flux_hbm,
    proj_hbm,
    rot_hbm,
    stress_hbm,
    cluster_hbm,
    orient_hbm,
    slot_hbm,
    send_map_hbm,
    out,
    state,
    stiff,
    jac,
    flux,
    proj,
    rot,
    stress,
    cluster,
    orient,
    slot,
    send_map,
    load_sem,
    w_der,
    w_vol,
    w_proj,
    w_lift,
    w_rot,
    padded,
    padded_rot,
    jac_wide,
    flux_wide,
    spare,
    picks,
    packs,
    mats_a,
    mats_b,
    first,
    second,
    middle,
    fine_first,
    table_one,
    table_two,
    picked,
    near,
    moved,
    rows,
    lines,
    slot_flux,
    slot_turn,
    turned,
    sums,
    far_in,
    lift_in,
    send_a,
    send_b,
    send_c,
    send_d,
    recv_a,
    recv_b,
    recv_c,
    recv_d,
    kept,
    send_sem,
    recv_sem,
    n_dom,
    n_sub,
):
    loads = {
        name: pltpu.make_async_copy(source, target, load_sem.at[index])
        for index, (name, source, target) in enumerate(
            (
                ("stiff", stiff_hbm, stiff),
                ("state", state_hbm, state),
                ("jac", jac_hbm, jac),
                ("proj", proj_hbm, proj),
                ("send_map", send_map_hbm, send_map),
                ("flux", flux_hbm, flux),
                ("slot", slot_hbm, slot),
                ("rot", rot_hbm, rot),
                ("orient", orient_hbm, orient),
                ("cluster", cluster_hbm, cluster),
                ("stress", stress_hbm, stress),
            )
        )
    }
    for load in loads.values():
        load.start()
    i, j = lax.axis_index("dom"), lax.axis_index("sub")
    links = (
        (i > 0, {"dom": i - 1}, 1),
        (i < n_dom - 1, {"dom": i + 1}, 0),
        (j > 0, {"sub": j - 1}, 3),
        (j < n_sub - 1, {"sub": j + 1}, 2),
    )
    sends = (send_a, send_b, send_c, send_d)
    recvs = (recv_a, recv_b, recv_c, recv_d)
    barrier = pltpu.get_barrier_semaphore()
    for there, device, _ in links:

        @pl.when(there)
        def _():
            pl.semaphore_signal(barrier, inc=1, device_id=device, device_id_type=MESH)

    def copy(stage, t):
        return pltpu.make_async_remote_copy(
            src_ref=sends[t].at[stage],
            dst_ref=recvs[links[t][2]].at[stage],
            send_sem=send_sem.at[stage, t],
            recv_sem=recv_sem.at[stage, links[t][2]],
            device_id=links[t][1],
            device_id_type=MESH,
        )

    def arrival(stage, t):
        return pltpu.make_async_remote_copy(
            src_ref=sends[t].at[stage],
            dst_ref=recvs[t].at[stage],
            send_sem=send_sem.at[stage, t],
            recv_sem=recv_sem.at[stage, t],
            device_id=links[t][1],
            device_id_type=MESH,
        )

    def start(stage):
        for t in range(4):

            @pl.when(links[t][0])
            def _():
                copy(stage, t).start()

    def finish(stage):
        for t in range(4):

            @pl.when(links[t][0])
            def _():
                arrival(stage, t).wait_recv()

    for t in range(4):

        @pl.when(jnp.logical_not(links[t][0]))
        def _():
            recvs[t][...] = jnp.zeros_like(recvs[t])

    mats = (mats_a, mats_b)
    for name in ("stiff", "state", "jac", "proj", "send_map"):
        loads[name].wait()
    prepare_derive(stiff, w_der)
    spread_jacobians(jac, jac_wide)
    prepare_faces(proj, w_proj, padded)
    pack_columns(send_map, spare, packs)

    def project_one(block):
        project([first[p] for p in block], block, w_proj, table_one)

    predict(state, w_der, jac_wide, mats, first, kept, project_one)
    both = pick_local(table_one, picks, packs, [s.at[0] for s in sends], picked)
    peers = sum(there.astype(jnp.int32) for there, _, _ in links)
    pl.semaphore_wait(barrier, peers)
    start(0)
    for name in ("flux", "slot", "rot", "orient", "cluster", "stress"):
        loads[name].wait()
    later(state, kept, second)
    prepare_volume(stiff, w_vol)
    pick_columns(slot, picks)
    spread_flux(flux, flux_wide)
    w_lift[...] = split_lift(padded[...])
    prepare_turn(rot, w_rot, padded_rot)
    prepare_slots(flux, orient, picks, rows, lines, slot_flux, slot_turn)
    picked[...] = dot(both, picks[0:LANES, :])
    fine = jnp.broadcast_to(cluster[...], (NB, NE)) == 0

    def volume(field, base, target):
        for block in BLOCKS:
            apply_stiffness(w_vol, [field(p) for p in block], mats_a, block[0], len(block))
        for block in BLOCKS:
            for p, x in zip(block, mix(mats_a, jac_wide, block)):
                target[p] = base(p) + x

    def local_update(table, target):
        for q in range(NQ):
            for f, x in enumerate(turn(picked, w_rot, orient, q)):
                near[q, f] = x
        for f in range(NF):
            totals = flux_term(
                lambda q: table[q * MP : (q + 1) * MP, f * NE : (f + 1) * NE], flux_wide, 0, f, None
            )
            totals = flux_term(lambda q: near[q, f], flux_wide, 1, f, totals)
            for p in range(NQ):
                lift_in[f * 3 * MP : (f + 1) * 3 * MP, p * NE : (p + 1) * NE] = split_rows(
                    flat(totals[p])
                )
        lifted = dot(w_lift[...], lift_in[...])
        for p in range(NQ):
            target[p] = target[p] - lifted[:, p * NE : (p + 1) * NE]

    def from_far(stage):
        return far_update(
            [r.at[stage] for r in recvs],
            w_rot,
            w_lift,
            picks,
            slot_flux,
            slot_turn,
            turned,
            sums,
            far_in,
        )

    volume(lambda p: first[p], lambda p: state[p], moved)
    local_update(table_one, moved)
    finish(0)
    lifted = from_far(0)
    for p in range(NQ):
        x = moved[p] - lifted[:, p * NE : (p + 1) * NE]
        moved[p] = x
        middle[p] = jnp.where(fine, x, state[p])

    def project_two(block):
        late = [jnp.where(fine, fine_first[p], second[p]) for p in block]
        for p, x in zip(block, late):
            second[p] = x
        project(late, block, w_proj, table_two)

    predict(middle, w_der, jac_wide, mats, fine_first, None, project_two)
    both = pick_local(table_two, picks, packs, [s.at[1] for s in sends], picked)
    start(1)
    picked[...] = dot(both, picks[0:LANES, :])
    volume(lambda p: second[p], lambda p: moved[p], moved)
    local_update(table_two, moved)
    finish(1)
    lifted = from_far(1)
    stepped = [moved[p] - lifted[:, p * NE : (p + 1) * NE] for p in range(NQ)]
    mean = (stepped[0] + stepped[1] + stepped[2]) / 3.0
    spread = [stepped[p] - mean for p in range(3)]
    lead = [s[0:1] for s in spread] + [stepped[p][0:1] for p in range(3, 6)]
    second_inv = (
        0.5 * (lead[0] * lead[0] + lead[1] * lead[1] + lead[2] * lead[2])
        + lead[3] * lead[3]
        + lead[4] * lead[4]
        + lead[5] * lead[5]
    )
    limit = stress[...]
    scaling = jnp.broadcast_to(limit / jnp.maximum(jnp.sqrt(second_inv), limit), (NB, NE))
    for p in range(3):
        out[p] = mean + scaling * spread[p]
        out[3 + p] = scaling * stepped[3 + p]
        out[6 + p] = stepped[6 + p]
    for t in range(4):

        @pl.when(links[t][0])
        def _():
            for stage in range(2):
                copy(stage, t).wait_send()


def on_device(n_dom, n_sub, modal_state, stiffness, jacobians, flux_solvers, projector, rotations, yield_stress, cluster, orient, neighbour_slot, send_map):
    vmem = pl.BlockSpec(memory_space=pltpu.VMEM)
    hbm = pl.BlockSpec(memory_space=pltpu.HBM)
    field = pltpu.VMEM((NQ, NB, NE), F32)

    def body(*refs):
        kernel(*refs, n_dom, n_sub)

    wide = lambda x: pltpu.with_memory_space_constraint(x, pltpu.HBM)
    result = pl.pallas_call(
        body,
        out_shape=jax.ShapeDtypeStruct((NQ, NB, NE), F32),
        in_specs=[hbm] * 11,
        out_specs=vmem,
        scratch_shapes=[
            pltpu.VMEM((NQ, NB, NE), F32),
            pltpu.VMEM((3, NB, NB), F32),
            pltpu.VMEM((NQ, NQ, 3, NE), F32),
            pltpu.VMEM((2, NQ, NQ, NF, NE), F32),
            pltpu.VMEM((NM, NF, NB), F32),
            pltpu.VMEM((3, NM, NM), F32),
            pltpu.VMEM((1, NE), F32),
            pltpu.VMEM((1, NE), jnp.int32),
            pltpu.VMEM((NF, NE), jnp.int32),
            pltpu.VMEM((NF, NE), jnp.int32),
            pltpu.VMEM((1, 2 * SLOTS_DOM + 2 * SLOTS_SUB), jnp.int32),
            pltpu.SemaphoreType.DMA((11,)),
            pltpu.VMEM((3 * NB, 3 * NB), BF16),
            pltpu.VMEM((3 * NB, 3 * NB), BF16),
            pltpu.VMEM((NF * MP, 3 * NB), BF16),
            pltpu.VMEM((NB, 3 * NF * MP), BF16),
            pltpu.VMEM((3 * MP, 3 * MP), BF16),
            pltpu.VMEM((NF * MP, NB), F32),
            pltpu.VMEM((3 * MP, MP), F32),
            pltpu.VMEM((NQ * NQ * 3, 8, NE), F32),
            pltpu.VMEM((2 * NF * NQ * NQ, 8, NE), F32),
            pltpu.VMEM((8, NE), jnp.int32),
            pltpu.VMEM((LANES + 2 * NE, LANES), BF16),
            pltpu.VMEM((LANES, LANES), BF16),
            pltpu.VMEM((3 * NB, NQ * NE), F32),
            pltpu.VMEM((3 * NB, NQ * NE), F32),
            field,
            field,
            field,
            field,
            pltpu.VMEM((ROWS, LANES), F32),
            pltpu.VMEM((ROWS, LANES), F32),
            pltpu.VMEM((2 * ROWS, LANES), F32),
            pltpu.VMEM((NQ, NF, MP, NE), F32),
            field,
            pltpu.VMEM((88, LANES), F32),
            pltpu.VMEM((8, LANES), F32),
            pltpu.VMEM((NQ * NQ, 8, 2 * NE), F32),
            pltpu.VMEM((8, 2 * NE), F32),
            pltpu.VMEM((NQ, MP, 2 * NE), F32),
            pltpu.VMEM((ROWS, 2 * NE), F32),
            pltpu.VMEM((3 * NF * MP, NQ * NE), BF16),
            pltpu.VMEM((3 * NF * MP, NQ * NE), BF16),
            pltpu.VMEM((2, HALF, NE), F32),
            pltpu.VMEM((2, HALF, NE), F32),
            pltpu.VMEM((2, QUARTER, NE), F32),
            pltpu.VMEM((2, QUARTER, NE), F32),
            pltpu.VMEM((2, HALF, NE), F32),
            pltpu.VMEM((2, HALF, NE), F32),
            pltpu.VMEM((2, QUARTER, NE), F32),
            pltpu.VMEM((2, QUARTER, NE), F32),
            pltpu.VMEM((ORDER - 1, NQ, NB, NE), F32),
            pltpu.SemaphoreType.DMA((2, 4)),
            pltpu.SemaphoreType.DMA((2, 4)),
        ],
        compiler_params=pltpu.CompilerParams(
            collective_id=0, has_side_effects=True, vmem_limit_bytes=48 << 20
        ),
    )(*map(wide, (
        jnp.transpose(modal_state, (1, 0, 2)),
        stiffness,
        jnp.transpose(jacobians, (1, 2, 0, 3)),
        jnp.transpose(flux_solvers, (0, 2, 3, 1, 4)),
        jnp.transpose(projector, (1, 0, 2)),
        rotations,
        yield_stress.reshape(1, -1),
        cluster.reshape(1, -1),
        orient,
        neighbour_slot,
        send_map.reshape(1, -1),
    )))
    return jnp.transpose(result, (1, 0, 2))


def solution(mesh):
    both = ("dom", "sub")
    n_dom, n_sub = mesh.shape["dom"], mesh.shape["sub"]
    placed = (
        P(None, None, both),
        P(),
        P(None, None, None, both),
        P(None, None, None, None, both),
        P(),
        P(),
        P(both),
        P(both),
        P(None, both),
        P(None, both),
        P(both),
    )

    def step(*args):
        return on_device(n_dom, n_sub, *args)

    return jax.shard_map(
        step, mesh=mesh, in_specs=placed, out_specs=P(None, None, both), check_vma=False
    )
```

```python
import math

import jax
import jax.numpy as jnp
from jax import lax
from jax.experimental import pallas as pl
from jax.experimental.pallas import tpu as pltpu
from jax.sharding import PartitionSpec as P

ORDER = 6
NB = 56
NQ = 9
NM = 21
MP = 24
NF = 4
NE = 128
SLOTS_DOM = 64
SLOTS_SUB = 32
ROWS = NQ * MP
LANES = NF * NE
HALF = 112
QUARTER = 64
MESH = pl.DeviceIdType.MESH
F32 = jnp.float32
BF16 = jnp.bfloat16


def dot(a, b):
    return jnp.dot(a, b, preferred_element_type=F32)


def dot_t(a, b):
    return lax.dot_general(a, b, (((0,), (0,)), ((), ())), preferred_element_type=F32)


def dot_rows(a, b):
    return lax.dot_general(a, b, (((1,), (1,)), ((), ())), preferred_element_type=F32)


def halves(x):
    high = x.astype(BF16).astype(F32)
    return high, x - high


def split_rows(x):
    high, low = halves(x)
    return jnp.concatenate([high, low, high], axis=0).astype(BF16)


def iota(shape, dim):
    return lax.broadcasted_iota(jnp.int32, shape, dim)


def as_bf16(mask):
    return jnp.where(mask, 1.0, 0.0).astype(BF16)


def split_weights(w):
    k = w.shape[1]
    high, low = halves(w)
    row, col = iota((k, 3 * k), 0), iota((k, 3 * k), 1)
    twice = as_bf16((col == row) | (col == row + k))
    once = as_bf16(col == row + 2 * k)
    return (dot(high.astype(BF16), twice) + dot(low.astype(BF16), once)).astype(BF16)


def split_weights_t(w):
    k = w.shape[0]
    high, low = halves(w)
    row, col = iota((k, 3 * k), 0), iota((k, 3 * k), 1)
    twice = as_bf16((col == row) | (col == row + k))
    once = as_bf16(col == row + 2 * k)
    return (dot_t(high.astype(BF16), twice) + dot_t(low.astype(BF16), once)).astype(BF16)


def split_lift(w):
    high, low = halves(w)
    rows, cols = NF * MP, 3 * NF * MP
    row, col = iota((rows, cols), 0), iota((rows, cols), 1)
    face = (
        (row >= MP).astype(jnp.int32)
        + (row >= 2 * MP).astype(jnp.int32)
        + (row >= 3 * MP).astype(jnp.int32)
    )
    start = row + 2 * MP * face
    twice = as_bf16((col == start) | (col == start + MP))
    once = as_bf16(col == start + 2 * MP)
    return (dot_t(high.astype(BF16), twice) + dot_t(low.astype(BF16), once)).astype(BF16)


def tiles(x):
    return x.reshape(x.shape[0] // 8, 8, x.shape[1])


def flat(x):
    return x.reshape(x.shape[0] * 8, x.shape[2])


def prepare_derive(stiff, w_der):
    for d in range(3):
        w_der[d * NB : (d + 1) * NB, :] = split_weights(stiff[d])


def prepare_volume(stiff, w_vol):
    for d in range(3):
        w_vol[d * NB : (d + 1) * NB, :] = split_weights_t(stiff[d])


def prepare_faces(proj, w_proj, padded):
    padded[...] = jnp.zeros_like(padded)
    for m in range(NM):
        for f in range(NF):
            padded[f * MP + m : f * MP + m + 1, :] = proj[m, f : f + 1, :]
    w_proj[...] = split_weights(padded[...])


def prepare_turn(rot, w_rot, padded_rot):
    padded_rot[...] = jnp.zeros_like(padded_rot)
    for o in range(3):
        padded_rot[o * MP : o * MP + NM, 0:NM] = rot[o]
    w_rot[...] = split_weights(padded_rot[...])


def spread_jacobians(jac, jac_wide):
    for q in range(NQ):
        for p in range(NQ):
            for d in range(3):
                jac_wide[(q * NQ + p) * 3 + d] = jnp.broadcast_to(jac[q, p, d : d + 1, :], (8, NE))


def spread_flux(flux, flux_wide):
    for q in range(NQ):
        for p in range(NQ):
            for s in range(2):
                for f in range(NF):
                    flux_wide[((s * NF + f) * NQ + q) * NQ + p] = jnp.broadcast_to(
                        flux[s, q, p, f : f + 1, :], (8, NE)
                    )


def pick_columns(slot, picks):
    rows = picks.shape[0]
    for f in range(NF):
        picks[:, f * NE : (f + 1) * NE] = as_bf16(
            iota((rows, NE), 0) == jnp.broadcast_to(slot[f : f + 1, :], (rows, NE))
        )


def pack_columns(send_map, spare, packs):
    spare[...] = jnp.full((8, NE), -1, jnp.int32)
    spare[0:1, 0:64] = send_map[0:1, NE : NE + 64]
    for t, want in enumerate((send_map[0:1, 0:NE], spare[0:1, :])):
        packs[:, t * NE : (t + 1) * NE] = as_bf16(
            iota((LANES, NE), 0) == jnp.broadcast_to(want, (LANES, NE))
        )


def apply_stiffness(weights, fields, out, start, count):
    rhs = jnp.concatenate([split_rows(fields[i]) for i in range(count)], axis=1)
    out[:, start * NE : (start + count) * NE] = dot(weights[...], rhs)


def mix(mats, jac_wide, block):
    totals = [None] * len(block)
    for q in range(NQ):
        for d in range(3):
            t = tiles(mats[d * NB : (d + 1) * NB, q * NE : (q + 1) * NE])
            for i, p in enumerate(block):
                term = t * jac_wide[(q * NQ + p) * 3 + d][None]
                totals[i] = term if totals[i] is None else totals[i] + term
    return [flat(t) for t in totals]


BLOCKS = ((0, 1), (2, 3), (4, 5), (6, 7), (8,))


ONES = [1.0 / math.factorial(k + 1) for k in range(ORDER)]
TWOS = [(2.0 ** (k + 1) - 1.0) / math.factorial(k + 1) for k in range(ORDER)]


def predict(state, w_der, jac_wide, mats, one, kept, done):
    for block in BLOCKS:
        fields = [state[p] for p in block]
        for p, x in zip(block, fields):
            one[p] = x
        apply_stiffness(w_der, fields, mats[0], block[0], len(block))

    for k in range(1, ORDER):
        source, target = mats[(k + 1) % 2], mats[k % 2]
        for block in BLOCKS:
            fields = mix(source, jac_wide, block)
            for p, x in zip(block, fields):
                one[p] = one[p] + ONES[k] * x
                if kept is not None:
                    kept[k - 1, p] = x
            if k + 1 < ORDER:
                apply_stiffness(w_der, fields, target, block[0], len(block))
            else:
                done(block)


def later(state, kept, two):
    for p in range(NQ):
        total = state[p]
        for k in range(1, ORDER):
            total = total + TWOS[k] * kept[k - 1, p]
        two[p] = total


def project(fields, block, w_proj, table):
    rhs = jnp.concatenate([split_rows(x) for x in fields], axis=1)
    faces = dot(w_proj[...], rhs)
    for i, p in enumerate(block):
        for f in range(NF):
            table[p * MP : (p + 1) * MP, f * NE : (f + 1) * NE] = faces[
                f * MP : (f + 1) * MP, i * NE : (i + 1) * NE
            ]


def pick_local(table, packs, packed):
    high, low = halves(table[...])
    both = jnp.concatenate([high, low], axis=0).astype(BF16)
    got = dot(both, packs[...])
    rows = got[0:ROWS] + got[ROWS : 2 * ROWS]
    rows = jnp.concatenate([rows, jnp.zeros((256 - ROWS, 2 * NE), F32)], axis=0)
    lane = iota((HALF, NE), 1)
    top, bottom = rows[0:HALF, 0:NE], rows[HALF : 2 * HALF, 0:NE]
    packed[0][...] = jnp.where(lane < 64, top, pltpu.roll(bottom, 64, 1))
    packed[1][...] = jnp.where(lane < 64, pltpu.roll(top, 64, 1), bottom)
    lane = iota((QUARTER, NE), 1)
    parts = [rows[QUARTER * k : QUARTER * (k + 1), NE : 2 * NE] for k in range(4)]
    for t in range(2):
        g = [
            x if k == t else pltpu.roll(x, (32 * k - 32 * t) % 128, 1)
            for k, x in enumerate(parts)
        ]
        packed[2 + t][...] = jnp.where(
            lane < 64, jnp.where(lane < 32, g[0], g[1]), jnp.where(lane < 96, g[2], g[3])
        )
    return both


def far_rows(got):
    near_low, near_high, side_low, side_high = [g[...] for g in got]
    lane = iota((HALF, NE), 1)
    top = jnp.where(lane < 64, near_low, pltpu.roll(near_high, 64, 1))
    bottom = jnp.where(lane < 64, pltpu.roll(near_low, 64, 1), near_high)
    dom = jnp.concatenate([top, bottom], axis=0)[0:ROWS]
    lane = iota((QUARTER, NE), 1)
    parts = []
    for k in range(4):
        a = side_low if k == 0 else pltpu.roll(side_low, (128 - 32 * k) % 128, 1)
        b = side_high if k == 1 else pltpu.roll(side_high, (160 - 32 * k) % 128, 1)
        parts.append(jnp.where(lane < 32, a, b))
    sub = jnp.concatenate(parts, axis=0)[0:ROWS]
    far = jnp.concatenate([dom, sub], axis=1)
    return halves(far)


def prepare_slots(flux, orient, picks, rows, lines, slot_flux, slot_turn):
    rows[80:88, :] = jnp.zeros((8, LANES), F32)
    for q in range(NQ):
        for p in range(NQ):
            for f in range(NF):
                rows[q * NQ + p : q * NQ + p + 1, f * NE : (f + 1) * NE] = flux[
                    1, q, p, f : f + 1, :
                ]
    high, low = halves(rows[...])
    both = jnp.concatenate([high, low], axis=0).astype(BF16)
    far = picks[LANES : LANES + 2 * NE, :]
    got = dot_rows(both, far)
    for index in range(NQ * NQ):
        line = got[index : index + 1, :] + got[88 + index : 89 + index, :]
        slot_flux[index] = jnp.broadcast_to(line, (8, 2 * NE))
    for f in range(NF):
        lines[:, f * NE : (f + 1) * NE] = jnp.broadcast_to(
            orient[f : f + 1, :].astype(F32), (8, NE)
        )
    slot_turn[...] = dot_rows(lines[...].astype(BF16), far)


def far_update(got, w_rot, w_lift, picks, slot_flux, slot_turn, turned, sums, lift_in):
    high, low = far_rows(got)
    which = slot_turn[...][None]
    for q in range(NQ):
        h, l = high[q * MP : (q + 1) * MP], low[q * MP : (q + 1) * MP]
        r = dot(w_rot[...], jnp.concatenate([h, l, h], axis=0).astype(BF16))
        r = [tiles(r[o * MP : (o + 1) * MP]) for o in range(3)]
        turned[q] = flat(jnp.where(which < 0.5, r[0], jnp.where(which < 1.5, r[1], r[2])))
    for block in ((0, 1, 2), (3, 4, 5), (6, 7, 8)):
        totals = [None] * len(block)
        for q in range(NQ):
            x = tiles(turned[q])
            for i, p in enumerate(block):
                term = x * slot_flux[q * NQ + p][None]
                totals[i] = term if totals[i] is None else totals[i] + term
        for i, p in enumerate(block):
            sums[p * MP : (p + 1) * MP, :] = flat(totals[i])
    high, low = halves(sums[...])
    both = jnp.concatenate([high, low], axis=0).astype(BF16)
    back = dot(both, picks[LANES : LANES + 2 * NE, :])
    for f in range(NF):
        c = slice(f * NE, (f + 1) * NE)
        for p in range(NQ):
            h = back[p * MP : (p + 1) * MP, c]
            l = back[ROWS + p * MP : ROWS + (p + 1) * MP, c]
            lift_in[f * 3 * MP : (f + 1) * 3 * MP, p * NE : (p + 1) * NE] = jnp.concatenate(
                [h, l, h], axis=0
            ).astype(BF16)
    return dot(w_lift[...], lift_in[...])


def turn(picked, w_rot, orient, q):
    high = picked[q * MP : (q + 1) * MP, :]
    low = picked[ROWS + q * MP : ROWS + (q + 1) * MP, :]
    rhs = jnp.concatenate([high, low, high], axis=0).astype(BF16)
    turned = dot(w_rot[...], rhs)
    out = []
    for f in range(NF):
        which = jnp.broadcast_to(orient[f : f + 1, :], (MP, NE))
        c = slice(f * NE, (f + 1) * NE)
        out.append(
            jnp.where(
                which == 0,
                turned[0:MP, c],
                jnp.where(which == 1, turned[MP : 2 * MP, c], turned[2 * MP : 3 * MP, c]),
            )
        )
    return out


def flux_term(face, flux_wide, side, f, total):
    totals = total
    for q in range(NQ):
        x = tiles(face(q))
        new = []
        for p in range(NQ):
            term = x * flux_wide[((side * NF + f) * NQ + q) * NQ + p][None]
            new.append(term if totals is None else totals[p] + term)
        totals = new
    return totals


def kernel(
    state_hbm,
    stiff_hbm,
    jac_hbm,
    flux_hbm,
    proj_hbm,
    rot_hbm,
    stress_hbm,
    cluster_hbm,
    orient_hbm,
    slot_hbm,
    send_map_hbm,
    out,
    state,
    stiff,
    jac,
    flux,
    proj,
    rot,
    stress,
    cluster,
    orient,
    slot,
    send_map,
    load_sem,
    w_der,
    w_vol,
    w_proj,
    w_lift,
    w_rot,
    padded,
    padded_rot,
    jac_wide,
    flux_wide,
    spare,
    picks,
    packs,
    mats_a,
    mats_b,
    first,
    second,
    middle,
    fine_first,
    table_one,
    table_two,
    picked,
    near,
    moved,
    rows,
    lines,
    slot_flux,
    slot_turn,
    turned,
    sums,
    far_in,
    lift_in,
    send_a,
    send_b,
    send_c,
    send_d,
    recv_a,
    recv_b,
    recv_c,
    recv_d,
    kept,
    send_sem,
    recv_sem,
    n_dom,
    n_sub,
):
    loads = {
        name: pltpu.make_async_copy(source, target, load_sem.at[index])
        for index, (name, source, target) in enumerate(
            (
                ("stiff", stiff_hbm, stiff),
                ("state", state_hbm, state),
                ("jac", jac_hbm, jac),
                ("proj", proj_hbm, proj),
                ("send_map", send_map_hbm, send_map),
                ("flux", flux_hbm, flux),
                ("slot", slot_hbm, slot),
                ("rot", rot_hbm, rot),
                ("orient", orient_hbm, orient),
                ("cluster", cluster_hbm, cluster),
                ("stress", stress_hbm, stress),
            )
        )
    }
    for load in loads.values():
        load.start()
    i, j = lax.axis_index("dom"), lax.axis_index("sub")
    links = (
        (i > 0, {"dom": i - 1}, 1),
        (i < n_dom - 1, {"dom": i + 1}, 0),
        (j > 0, {"sub": j - 1}, 3),
        (j < n_sub - 1, {"sub": j + 1}, 2),
    )
    sends = (send_a, send_b, send_c, send_d)
    recvs = (recv_a, recv_b, recv_c, recv_d)
    barrier = pltpu.get_barrier_semaphore()
    for there, device, _ in links:

        @pl.when(there)
        def _():
            pl.semaphore_signal(barrier, inc=1, device_id=device, device_id_type=MESH)

    def copy(stage, t):
        return pltpu.make_async_remote_copy(
            src_ref=sends[t].at[stage],
            dst_ref=recvs[links[t][2]].at[stage],
            send_sem=send_sem.at[stage, t],
            recv_sem=recv_sem.at[stage, links[t][2]],
            device_id=links[t][1],
            device_id_type=MESH,
        )

    def arrival(stage, t):
        return pltpu.make_async_remote_copy(
            src_ref=sends[t].at[stage],
            dst_ref=recvs[t].at[stage],
            send_sem=send_sem.at[stage, t],
            recv_sem=recv_sem.at[stage, t],
            device_id=links[t][1],
            device_id_type=MESH,
        )

    def start(stage):
        for t in range(4):

            @pl.when(links[t][0])
            def _():
                copy(stage, t).start()

    def finish(stage):
        for t in range(4):

            @pl.when(links[t][0])
            def _():
                arrival(stage, t).wait_recv()

    for t in range(4):

        @pl.when(jnp.logical_not(links[t][0]))
        def _():
            recvs[t][...] = jnp.zeros_like(recvs[t])

    mats = (mats_a, mats_b)
    for name in ("stiff", "state", "jac", "proj", "send_map"):
        loads[name].wait()
    prepare_derive(stiff, w_der)
    spread_jacobians(jac, jac_wide)
    prepare_faces(proj, w_proj, padded)
    pack_columns(send_map, spare, packs)

    def project_one(block):
        project([first[p] for p in block], block, w_proj, table_one)

    predict(state, w_der, jac_wide, mats, first, kept, project_one)
    both = pick_local(table_one, packs, [s.at[0] for s in sends])
    peers = sum(there.astype(jnp.int32) for there, _, _ in links)
    pl.semaphore_wait(barrier, peers)
    start(0)
    for name in ("flux", "slot", "rot", "orient", "cluster", "stress"):
        loads[name].wait()
    later(state, kept, second)
    prepare_volume(stiff, w_vol)
    pick_columns(slot, picks)
    spread_flux(flux, flux_wide)
    w_lift[...] = split_lift(padded[...])
    prepare_turn(rot, w_rot, padded_rot)
    prepare_slots(flux, orient, picks, rows, lines, slot_flux, slot_turn)
    picked[...] = dot(both, picks[0:LANES, :])
    fine = jnp.broadcast_to(cluster[...], (NB, NE)) == 0

    def volume(field, base, target):
        for block in BLOCKS:
            apply_stiffness(w_vol, [field(p) for p in block], mats_a, block[0], len(block))
        for block in BLOCKS:
            for p, x in zip(block, mix(mats_a, jac_wide, block)):
                target[p] = base(p) + x

    def local_update(table, target):
        for q in range(NQ):
            for f, x in enumerate(turn(picked, w_rot, orient, q)):
                near[q, f] = x
        for f in range(NF):
            totals = flux_term(
                lambda q: table[q * MP : (q + 1) * MP, f * NE : (f + 1) * NE], flux_wide, 0, f, None
            )
            totals = flux_term(lambda q: near[q, f], flux_wide, 1, f, totals)
            for p in range(NQ):
                lift_in[f * 3 * MP : (f + 1) * 3 * MP, p * NE : (p + 1) * NE] = split_rows(
                    flat(totals[p])
                )
        lifted = dot(w_lift[...], lift_in[...])
        for p in range(NQ):
            target[p] = target[p] - lifted[:, p * NE : (p + 1) * NE]

    def from_far(stage):
        return far_update(
            [r.at[stage] for r in recvs],
            w_rot,
            w_lift,
            picks,
            slot_flux,
            slot_turn,
            turned,
            sums,
            far_in,
        )

    volume(lambda p: first[p], lambda p: state[p], moved)
    local_update(table_one, moved)
    finish(0)
    lifted = from_far(0)
    for p in range(NQ):
        x = moved[p] - lifted[:, p * NE : (p + 1) * NE]
        moved[p] = x
        middle[p] = jnp.where(fine, x, state[p])

    def project_two(block):
        late = [jnp.where(fine, fine_first[p], second[p]) for p in block]
        for p, x in zip(block, late):
            second[p] = x
        project(late, block, w_proj, table_two)

    predict(middle, w_der, jac_wide, mats, fine_first, None, project_two)
    both = pick_local(table_two, packs, [s.at[1] for s in sends])
    start(1)
    picked[...] = dot(both, picks[0:LANES, :])
    volume(lambda p: second[p], lambda p: moved[p], moved)
    local_update(table_two, moved)
    finish(1)
    lifted = from_far(1)
    stepped = [moved[p] - lifted[:, p * NE : (p + 1) * NE] for p in range(NQ)]
    mean = (stepped[0] + stepped[1] + stepped[2]) / 3.0
    spread = [stepped[p] - mean for p in range(3)]
    lead = [s[0:1] for s in spread] + [stepped[p][0:1] for p in range(3, 6)]
    second_inv = (
        0.5 * (lead[0] * lead[0] + lead[1] * lead[1] + lead[2] * lead[2])
        + lead[3] * lead[3]
        + lead[4] * lead[4]
        + lead[5] * lead[5]
    )
    limit = stress[...]
    scaling = jnp.broadcast_to(limit / jnp.maximum(jnp.sqrt(second_inv), limit), (NB, NE))
    for p in range(3):
        out[p] = mean + scaling * spread[p]
        out[3 + p] = scaling * stepped[3 + p]
        out[6 + p] = stepped[6 + p]
    for t in range(4):

        @pl.when(links[t][0])
        def _():
            for stage in range(2):
                copy(stage, t).wait_send()


def on_device(n_dom, n_sub, modal_state, stiffness, jacobians, flux_solvers, projector, rotations, yield_stress, cluster, orient, neighbour_slot, send_map):
    vmem = pl.BlockSpec(memory_space=pltpu.VMEM)
    hbm = pl.BlockSpec(memory_space=pltpu.HBM)
    field = pltpu.VMEM((NQ, NB, NE), F32)

    def body(*refs):
        kernel(*refs, n_dom, n_sub)

    wide = lambda x: pltpu.with_memory_space_constraint(x, pltpu.HBM)
    result = pl.pallas_call(
        body,
        out_shape=jax.ShapeDtypeStruct((NQ, NB, NE), F32),
        in_specs=[hbm] * 11,
        out_specs=vmem,
        scratch_shapes=[
            pltpu.VMEM((NQ, NB, NE), F32),
            pltpu.VMEM((3, NB, NB), F32),
            pltpu.VMEM((NQ, NQ, 3, NE), F32),
            pltpu.VMEM((2, NQ, NQ, NF, NE), F32),
            pltpu.VMEM((NM, NF, NB), F32),
            pltpu.VMEM((3, NM, NM), F32),
            pltpu.VMEM((1, NE), F32),
            pltpu.VMEM((1, NE), jnp.int32),
            pltpu.VMEM((NF, NE), jnp.int32),
            pltpu.VMEM((NF, NE), jnp.int32),
            pltpu.VMEM((1, 2 * SLOTS_DOM + 2 * SLOTS_SUB), jnp.int32),
            pltpu.SemaphoreType.DMA((11,)),
            pltpu.VMEM((3 * NB, 3 * NB), BF16),
            pltpu.VMEM((3 * NB, 3 * NB), BF16),
            pltpu.VMEM((NF * MP, 3 * NB), BF16),
            pltpu.VMEM((NB, 3 * NF * MP), BF16),
            pltpu.VMEM((3 * MP, 3 * MP), BF16),
            pltpu.VMEM((NF * MP, NB), F32),
            pltpu.VMEM((3 * MP, MP), F32),
            pltpu.VMEM((NQ * NQ * 3, 8, NE), F32),
            pltpu.VMEM((2 * NF * NQ * NQ, 8, NE), F32),
            pltpu.VMEM((8, NE), jnp.int32),
            pltpu.VMEM((LANES + 2 * NE, LANES), BF16),
            pltpu.VMEM((LANES, 2 * NE), BF16),
            pltpu.VMEM((3 * NB, NQ * NE), F32),
            pltpu.VMEM((3 * NB, NQ * NE), F32),
            field,
            field,
            field,
            field,
            pltpu.VMEM((ROWS, LANES), F32),
            pltpu.VMEM((ROWS, LANES), F32),
            pltpu.VMEM((2 * ROWS, LANES), F32),
            pltpu.VMEM((NQ, NF, MP, NE), F32),
            field,
            pltpu.VMEM((88, LANES), F32),
            pltpu.VMEM((8, LANES), F32),
            pltpu.VMEM((NQ * NQ, 8, 2 * NE), F32),
            pltpu.VMEM((8, 2 * NE), F32),
            pltpu.VMEM((NQ, MP, 2 * NE), F32),
            pltpu.VMEM((ROWS, 2 * NE), F32),
            pltpu.VMEM((3 * NF * MP, NQ * NE), BF16),
            pltpu.VMEM((3 * NF * MP, NQ * NE), BF16),
            pltpu.VMEM((2, HALF, NE), F32),
            pltpu.VMEM((2, HALF, NE), F32),
            pltpu.VMEM((2, QUARTER, NE), F32),
            pltpu.VMEM((2, QUARTER, NE), F32),
            pltpu.VMEM((2, HALF, NE), F32),
            pltpu.VMEM((2, HALF, NE), F32),
            pltpu.VMEM((2, QUARTER, NE), F32),
            pltpu.VMEM((2, QUARTER, NE), F32),
            pltpu.VMEM((ORDER - 1, NQ, NB, NE), F32),
            pltpu.SemaphoreType.DMA((2, 4)),
            pltpu.SemaphoreType.DMA((2, 4)),
        ],
        compiler_params=pltpu.CompilerParams(
            collective_id=0, has_side_effects=True, vmem_limit_bytes=48 << 20
        ),
    )(*map(wide, (
        jnp.transpose(modal_state, (1, 0, 2)),
        stiffness,
        jnp.transpose(jacobians, (1, 2, 0, 3)),
        jnp.transpose(flux_solvers, (0, 2, 3, 1, 4)),
        jnp.transpose(projector, (1, 0, 2)),
        rotations,
        yield_stress.reshape(1, -1),
        cluster.reshape(1, -1),
        orient,
        neighbour_slot,
        send_map.reshape(1, -1),
    )))
    return jnp.transpose(result, (1, 0, 2))


def solution(mesh):
    both = ("dom", "sub")
    n_dom, n_sub = mesh.shape["dom"], mesh.shape["sub"]
    placed = (
        P(None, None, both),
        P(),
        P(None, None, None, both),
        P(None, None, None, None, both),
        P(),
        P(),
        P(both),
        P(both),
        P(None, both),
        P(None, both),
        P(both),
    )

    def step(*args):
        return on_device(n_dom, n_sub, *args)

    return jax.shard_map(
        step, mesh=mesh, in_specs=placed, out_specs=P(None, None, both), check_vma=False
    )
```
